256 devices in a mesh: blk: 32 (over x_lo, z, core), rep: 8 (over x_hi, y).
Axes of the slice: x: 4 (x_hi: 2, x_lo: 2; x = x_hi * 2 + x_lo), y: 4, z: 8, core: 2. Of those that a mesh axis runs over, the one named last changes fastest.
Arguments:
- integrals: bfloat16 [32, 512, 1024], P('blk'), may hold values from -0.59765625 to 0.59765625
- eps_occ: float32 [32], replicated, may hold values from -2 to -0.5
- eps_vir: float32 [512], replicated, may hold values from 0.5 to 3
- offsets: int32 [16], P('rep'), may hold values from 0 to 15
Outputs:
- gamma: float32 [32, 512, 1024], P('blk', None, 'rep')
The draws below stay inside these ranges and needn't reach their ends.
All inputs are finite; a program needn't handle non-finite values.
Results may differ from the reference program's by a relative error of at most 0.0017.
Values may be sent and summed in bfloat16 or wider, within the bound.
A program may use at most 64 MiB of HBM per device.

```python
import jax
import jax.numpy as jnp
from jax import lax

V = 512
AUX = 1024
OCC = 32
PAIRS = 16


def with_ends(array, key, smallest, largest):
    longest = array.shape.index(max(array.shape))
    spots = []
    for shift in (0, 1):
        where = [jax.random.randint(jax.random.fold_in(key, axis), (), 0, length) for axis, length in enumerate(array.shape)]
        where[longest] = (where[longest] + shift) % array.shape[longest]
        spots.append(tuple(where))
    return array.at[spots[0]].set(smallest).at[spots[1]].set(largest)


def level_of(stream_key, dims, cuts, smallest, top_value):
    gain, own = 1.0, jax.random.fold_in(stream_key, 6)
    for dim, blocks in cuts:
        heights = jnp.exp(jax.random.uniform(jax.random.fold_in(own, dim), (blocks,), jnp.float32, smallest / len(cuts), top_value / len(cuts)))
        gain = gain * jnp.repeat(heights, dims[dim] // blocks).reshape([-1 if axis == dim else 1 for axis in range(len(dims))])
    return gain


def bell_draw(own_key, dims, scale, most, cuts=(), kind=jnp.bfloat16):
    factor_of = level_of(own_key, dims, cuts, -0.22, 0.18) if cuts else 1.0
    drawn = jax.random.normal(own_key, dims, jnp.float32) * scale * factor_of
    return jnp.minimum(jnp.maximum(drawn, -most), most).astype(kind)


def setup_inputs(seed: int = 0) -> dict:
    streams_of = jax.random.split(jax.random.key(seed), 5)
    return {
        "integrals": bell_draw(streams_of[0], (OCC, V, AUX), 0.1, 0.59765625, ((0, 32),)),
        "eps_occ": jnp.clip(jax.random.uniform(streams_of[1], (OCC,), jnp.float32, -2.0, -0.5), -2.0, -0.5),
        "eps_vir": jnp.clip(jax.random.uniform(streams_of[2], (V,), jnp.float32, 0.5, 3.0), 0.5, 3.0),
        "offsets": with_ends(jax.random.randint(streams_of[3], (PAIRS,), 0, PAIRS), jax.random.fold_in(streams_of[3], 1), 0, PAIRS - 1).astype(jnp.int32),
    }


def reference(integrals, eps_occ, eps_vir, offsets):
    whole = integrals.astype(jnp.float32)

    def step(total, shift):
        partner_tiles = jnp.roll(integrals, shift, axis=0).astype(jnp.float32)
        pair = jnp.einsum("iap,ibp->iab", whole, partner_tiles)
        e_partner = jnp.roll(eps_occ, shift)
        denom = eps_vir[None, :, None] + eps_vir[None, None, :] - eps_occ[:, None, None] - e_partner[:, None, None]
        amp = (-pair / denom).astype(jnp.bfloat16).astype(jnp.float32)
        own = jnp.einsum("iab,ibp->iap", amp, partner_tiles)
        part = jnp.einsum("iab,iap->ibp", amp, whole)
        part = lax.optimization_barrier(part.astype(jnp.bfloat16)).astype(jnp.float32)
        total = total + own + jnp.roll(part, -shift, axis=0)
        return total, None

    start = jnp.zeros(integrals.shape, jnp.float32)
    gamma, unused = lax.scan(step, start, offsets)
    return gamma
```

```python
import functools

import jax
import jax.numpy as jnp
from jax import lax
from jax.experimental import pallas as pl
from jax.experimental.pallas import tpu as pltpu
from jax.sharding import PartitionSpec as P

MESH = pl.DeviceIdType.MESH
F32 = jnp.float32
BF16 = jnp.bfloat16

NZ, NY, NX = 8, 4, 4
ORBS = 32
SIGNS = (1, 2, 2, 2, 1)
BASES = (0, 256, 768, 1280, 1792)
ROWS = (256, 512, 512, 512, 256)
SUB = 32


def row_of(g, par, kind, sgn, q):
    return BASES[g] + ((par * 2 + kind) * SIGNS[g] + sgn) * 64 + SUB * q


def entries_of(g):
    out = []
    for par in range(2):
        for kind in range(2):
            for sgn in range(SIGNS[g]):
                out.append((par, kind, g if sgn else -g))
    return out


class Copies:
    def __init__(self, send_sem, recv_sem):
        self.send_sem, self.recv_sem = send_sem, recv_sem
        self.made = {}

    def start(self, name, src, dst, device):
        n = len(self.made)
        copy = pltpu.make_async_remote_copy(
            src_ref=src, dst_ref=dst, send_sem=self.send_sem.at[n],
            recv_sem=self.recv_sem.at[n], device_id=device, device_id_type=MESH,
        )
        self.made[name] = copy
        copy.start()

    def arrived(self, name):
        self.made[name].wait_recv()

    def finish(self):
        for copy in self.made.values():
            copy.wait_send()


N_COPIES = 96


def kernel(b_ref, ev_ref, eo_ref, off_ref, out_ref, g_ref, inv_ref, ct_ref, w_ref, evc_ref, amp_ref,
           acc_ref, sb_ref, offb_ref, offr_ref, ry_ref, rly_ref, rx_ref, rlx_ref, t2_ref, rl2_ref,
           rx2_ref, t3_ref, rl3_ref, ry2_ref, send_sem, recv_sem, local_sem):
    blk = lax.axis_index("blk")
    rep = lax.axis_index("rep")
    core = lax.rem(blk, 2)
    z = lax.rem(lax.div(blk, 2), NZ)
    x_lo = lax.div(blk, 2 * NZ)
    y = lax.rem(rep, NY)
    x_hi = lax.div(rep, NY)
    x = 2 * x_hi + x_lo

    def device(xx, yy, zz, cc):
        return (lax.rem(xx, 2) * (2 * NZ) + zz * 2 + cc, lax.div(xx, 2) * NY + yy)

    x_r, x_l = lax.rem(x + 1, NX), lax.rem(x + NX - 1, NX)
    y_r, y_l = lax.rem(y + 1, NY), lax.rem(y + NY - 1, NY)
    y_o = lax.rem(y + 2, NY)
    z_r, z_l = lax.rem(z + 1, NZ), lax.rem(z + NZ - 1, NZ)
    zs = (device(x, y, z_r, core), device(x, y, z_l, core))
    xs = (device(x_r, y, z, core), device(x_l, y, z, core))
    ys = (device(x, y_r, z, core), device(x, y_l, z, core))
    sib = device(x, y, z, 1 - core)

    rows8 = lax.broadcasted_iota(jnp.int32, (8, 128), 0)
    offb_ref[0] = jnp.where(rows8 == 0, off_ref[0], jnp.where(rows8 == 1, off_ref[1], -1))

    barrier = pltpu.get_barrier_semaphore()
    for who in (*zs, *xs, *ys, sib):
        pl.semaphore_signal(barrier, inc=1, device_id=who, device_id_type=MESH)
    pl.semaphore_wait(barrier, 7)

    copies = Copies(send_sem, recv_sem)
    mine = pl.multiple_of(128 * y + 64 * x_hi, 64)

    def same(g, sgn, q, count=1):
        if g == 0:
            return b_ref.at[pl.ds(mine + SUB * q, SUB * count), :]
        return g_ref.at[pl.ds(row_of(g, 0, 0, sgn, q), SUB * count), :]

    def slot(g, par, kind, sgn, q, count=1):
        return g_ref.at[pl.ds(row_of(g, par, kind, sgn, q), SUB * count), :]

    def z_send(d, s, q):
        sgn = d if SIGNS[s] == 2 else 0
        to = d if SIGNS[s + 1] == 2 else 0
        copies.start(("z", d, s, q), same(s, sgn, q), slot(s + 1, 0, 0, to, q), zs[d])

    def x_send(g, sgn, q):
        copies.start(("x", g, sgn, q), same(g, sgn, q), slot(g, 0, 1, sgn, q), xs[q])

    def sib_send(g, kind, sgn, q, count=1):
        src = same(g, sgn, q, count) if kind == 0 else slot(g, 0, 1, sgn, q, count)
        copies.start(("s", g, kind, sgn, q), src, slot(g, 1, kind, sgn, q, count), sib)

    for f in range(2):
        z_send(0, 0, f)
        z_send(1, 0, 1 - f)
    for q in range(2):
        x_send(0, 0, q)
    sib_send(0, 0, 0, 0, 2)
    for d in range(2):
        copies.start(("o", d), offb_ref.at[0], offb_ref.at[1 + d], ys[d])
    local = pltpu.make_async_copy(b_ref.at[pl.ds(mine, 64), :], slot(0, 0, 0, 0, 0, 2), local_sem)
    local.start()

    lanes = lax.broadcasted_iota(jnp.int32, (1, 128), 1)
    low = lanes < 64
    ev_y = ev_ref[:, pl.ds(pl.multiple_of(128 * y, 128), 128)]
    ev_swap = jnp.concatenate([ev_y[:, 64:], ev_y[:, :64]], axis=1)
    e_k = eo_ref[blk]
    half_of_lane = lax.div(lanes, 64)
    quarter = lax.rem(lax.div(lanes, SUB), 2)
    half_flip = jnp.where(quarter == 0, lax.div(x_l, 2), lax.div(x_r, 2))
    distances = []
    for g in range(5):
        ents = entries_of(g)
        for n in range(0, len(ents), 2):
            e_l, dist, half = [], [], []
            for par, kind, dz in ents[n:n + 2]:
                c = core if par == 0 else 1 - core
                xl = x_lo if kind == 0 else 1 - x_lo
                orb = xl * (2 * NZ) + lax.rem(z + dz + NZ, NZ) * 2 + c
                gap = lax.rem(blk - orb + ORBS, ORBS)
                e_l.append(eo_ref[orb])
                dist.append(jnp.minimum(gap, ORBS - gap))
                half.append(jnp.full((1, 128), x_hi, jnp.int32) if kind == 0 else half_flip)
            want = jnp.where(low, half[0], half[1])
            ev_b = jnp.where(want == half_of_lane, ev_y, ev_swap)
            col = BASES[g] + 64 * n
            ct_ref[:, col:col + 128] = ev_b - e_k - jnp.where(low, e_l[0], e_l[1])
            distances.append((col, jnp.where(low, dist[0], dist[1])))
    for n in range(4):
        tile = jnp.broadcast_to(ev_ref[:, 128 * n:128 * n + 128], (128, 128))
        evc_ref[128 * n:128 * n + 128, :] = tile.T

    def invert(i, carry):
        rows = pl.ds(pl.multiple_of(i * 32, 32), 32)
        ev_a = evc_ref[rows, :]
        for n in range(16):
            cols = slice(128 * n, 128 * n + 128)
            inv_ref[rows, cols] = -1.0 / (ev_a + ct_ref[:, cols])
        return carry

    lax.fori_loop(0, 16, invert, 0)

    def weigh():
        table = offb_ref[...].reshape(64, 128)
        for col, dist in distances:
            count = jnp.sum(jnp.where(table == dist, 1.0, 0.0), axis=0, keepdims=True)
            w_ref[:, col:col + 128] = jnp.where(dist == 0, 2.0 * count, count)

    def amplitudes(g):
        for n in range(ROWS[g] // 256):
            cols = slice(BASES[g] + 256 * n, BASES[g] + 256 * n + 256)
            right = g_ref[cols, :]
            weight = w_ref[:, cols]
            for m in range(2):
                rows = slice(256 * m, 256 * m + 256)
                pair = lax.dot_general(b_ref[rows, :], right, (((1,), (1,)), ((), ())),
                                       preferred_element_type=F32)
                amp_ref[rows, 256 * n:256 * n + 256] = (pair * (inv_ref[rows, cols] * weight)).astype(BF16)

    def contract(g, rows, final=False):
        for n in range(4):
            res = jnp.dot(amp_ref[rows, :ROWS[g]], g_ref[BASES[g]:BASES[g] + ROWS[g], 256 * n:256 * n + 256],
                          preferred_element_type=F32)
            for h in range(2):
                j = 2 * n + h
                xh, yy = j // NY, j % NY
                val = res[:, 128 * h:128 * h + 128]
                if g > 0:
                    val = val + acc_ref[yy, xh, rows, :]
                acc_ref[yy, xh, rows, :] = val
                if final:
                    sb_ref[yy, xh, rows, :] = val.astype(BF16)

    def group(g):
        for sgn in range(SIGNS[g]):
            if g == 0:
                copies.arrived(("s", 0, 0, 0, 0))
            else:
                for q in range(2):
                    copies.arrived(("s", g, 0, sgn, q))
            for q in range(2):
                copies.arrived(("s", g, 1, sgn, q))
        if g == 0:
            local.wait()
        amplitudes(g)

    def x_arrivals(g):
        for sgn in range(SIGNS[g]):
            for q in range(2):
                copies.arrived(("x", g, sgn, q))
                sib_send(g, 1, sgn, q)

    for s in range(1, 5):
        for f in range(2):
            if s == 4 and f == 1:
                continue
            for d in range(2):
                q = f if d == 0 else 1 - f
                copies.arrived(("z", d, s - 1, q))
                sgn = d if SIGNS[s] == 2 else 0
                if s < 3 or (s == 3 and f == 0):
                    z_send(d, s, q)
                x_send(s, sgn, q)
                sib_send(s, 0, sgn, q)
            if f == 0:
                x_arrivals(s - 1)
                if s == 1:
                    copies.arrived(("o", 0))
                    copies.start(("o", 2), offb_ref.at[1], offb_ref.at[3], ys[0])
                if s == 2:
                    copies.arrived(("ox", 0))
                    copies.start(("ox", 1), offr_ref, offb_ref.at[pl.ds(4, 4)], xs[0])
            if f == 1 and s == 1:
                copies.arrived(("o", 1))
                copies.arrived(("o", 2))
                copies.start(("ox", 0), offb_ref.at[pl.ds(0, 4)], offr_ref, xs[0])
        if s == 3:
            copies.arrived(("ox", 1))
            weigh()
            for g in range(2):
                group(g)
                contract(g, slice(0, 512))
        if s == 4:
            group(2)
            contract(2, slice(0, 512))
            group(3)
            contract(3, slice(0, 512))
    x_arrivals(4)
    group(4)

    lo, hi = slice(0, 256), slice(256, 512)
    other = 1 - x_hi
    contract(4, hi, True)
    for d in range(2):
        copies.start(("x1", d), sb_ref.at[pl.ds(2 * d, 2), other, pl.ds(256, 256), :], rlx_ref.at[d], xs[d])
    contract(4, lo, True)
    for d, to in enumerate((y_r, y_l)):
        copies.start(("y1r", d), sb_ref.at[y_o, d, pl.ds(0, 256), :], rly_ref.at[d], ys[d])
        copies.start(("y1", d), sb_ref.at[to, :, pl.ds(0, 256), :], ry_ref.at[d], ys[d])
    for d in range(2):
        copies.arrived(("x1", d))
        copies.start(("x1f", d), rlx_ref.at[d], rx_ref.at[pl.ds(2 * d, 2)], xs[d])
    for d in range(2):
        copies.arrived(("y1r", d))
        copies.start(("y1f", d), rly_ref.at[d], ry_ref.at[2, d], ys[d])
    for d in range(2):
        copies.arrived(("x1f", d))
    for yy in range(NY):
        t3_ref[yy] = (acc_ref[yy, x_hi, hi, :] + rx_ref[yy].astype(F32)).astype(BF16)
    for d, to in enumerate((y_r, y_l)):
        copies.start(("y2r", d), t3_ref.at[y_o, pl.ds(128 * d, 128), :], rl3_ref.at[d], ys[d])
        copies.start(("y2", d), t3_ref.at[to], ry2_ref.at[d], ys[d])
    for d in range(2):
        copies.arrived(("y1", d))
    for d in range(2):
        copies.arrived(("y1f", d))

    def y_sum(which):
        return (acc_ref[y, which, lo, :] + ry_ref[0, which].astype(F32) + ry_ref[1, which].astype(F32)
                + ry_ref[2, which].astype(F32))

    t2_ref[...] = y_sum(other).astype(BF16)
    for d in range(2):
        copies.start(("x2", d), t2_ref.at[pl.ds(128 * d, 128), :], rl2_ref.at[d], xs[d])
    for d in range(2):
        copies.arrived(("y2r", d))
        copies.start(("y2f", d), rl3_ref.at[d], ry2_ref.at[2, pl.ds(128 * d, 128), :], ys[d])
    for d in range(2):
        copies.arrived(("x2", d))
        copies.start(("x2f", d), rl2_ref.at[d], rx2_ref.at[pl.ds(128 * d, 128), :], xs[d])
    for d in range(2):
        copies.arrived(("y2", d))
    for d in range(2):
        copies.arrived(("y2f", d))
    out_ref[0, hi, :] = (acc_ref[y, x_hi, hi, :] + rx_ref[y].astype(F32) + ry2_ref[0].astype(F32)
                         + ry2_ref[1].astype(F32) + ry2_ref[2].astype(F32))
    for d in range(2):
        copies.arrived(("x2f", d))
    out_ref[0, lo, :] = y_sum(x_hi) + rx2_ref[...].astype(F32)
    copies.finish()


def per_device(integrals, eps_occ, eps_vir, offsets):
    v, aux = integrals.shape[1:]
    vmem = pl.BlockSpec(memory_space=pltpu.VMEM)
    smem = pl.BlockSpec(memory_space=pltpu.SMEM)
    return pl.pallas_call(
        kernel,
        out_shape=jax.ShapeDtypeStruct((1, v, aux // 8), F32),
        in_specs=[vmem, vmem, smem, smem],
        out_specs=vmem,
        scratch_shapes=[
            pltpu.VMEM((2048, aux), BF16),
            pltpu.VMEM((v, 2048), F32),
            pltpu.VMEM((1, 2048), F32),
            pltpu.VMEM((1, 2048), F32),
            pltpu.VMEM((v, 128), F32),
            pltpu.VMEM((v, 512), BF16),
            pltpu.VMEM((NY, 2, v, 128), F32),
            pltpu.VMEM((NY, 2, v, 128), BF16),
            pltpu.VMEM((8, 8, 128), jnp.int32),
            pltpu.VMEM((4, 8, 128), jnp.int32),
            pltpu.VMEM((3, 2, 256, 128), BF16),
            pltpu.VMEM((2, 256, 128), BF16),
            pltpu.VMEM((4, 256, 128), BF16),
            pltpu.VMEM((2, 2, 256, 128), BF16),
            pltpu.VMEM((256, 128), BF16),
            pltpu.VMEM((2, 128, 128), BF16),
            pltpu.VMEM((256, 128), BF16),
            pltpu.VMEM((NY, 256, 128), BF16),
            pltpu.VMEM((2, 128, 128), BF16),
            pltpu.VMEM((3, 256, 128), BF16),
            pltpu.SemaphoreType.DMA((N_COPIES,)),
            pltpu.SemaphoreType.DMA((N_COPIES,)),
            pltpu.SemaphoreType.DMA,
        ],
        compiler_params=pltpu.CompilerParams(
            collective_id=0, has_side_effects=True, vmem_limit_bytes=56 << 20
        ),
        name="pair_amplitudes",
    )(integrals[0], eps_vir[None, :], eps_occ, offsets)


def solution(mesh):
    in_specs = (P("blk", None, None), P(), P(), P("rep"))
    out_specs = P("blk", None, "rep")
    return jax.shard_map(
        per_device, mesh=mesh, in_specs=in_specs, out_specs=out_specs, check_vma=False
    )
```

```python
import jax
import jax.numpy as jnp
from jax import lax
from jax.experimental import pallas as pl
from jax.experimental.pallas import tpu as pltpu
from jax.sharding import PartitionSpec as P

MESH = pl.DeviceIdType.MESH
F32 = jnp.float32
BF16 = jnp.bfloat16

NZ, NY, NX = 8, 4, 4
ORBS = 32
PIECE = 16
BLOCK = 256


def row_of(g, par, kind, sgn, c):
    if g in (0, 4):
        entry = (0 if g == 0 else 28) + kind * 2 + par
    else:
        entry = 4 + (g - 1) * 8 + kind * 4 + par * 2 + sgn
    return entry * 64 + PIECE * c


def entry_list():
    out = [None] * 32
    for g in range(5):
        for par in range(2):
            for kind in range(2):
                for sgn in range(1 if g in (0, 4) else 2):
                    out[row_of(g, par, kind, sgn, 0) // 64] = (par, kind, g if sgn else -g)
    return out


class Copies:
    def __init__(self, send_sem, recv_sem):
        self.send_sem, self.recv_sem = send_sem, recv_sem
        self.made = {}

    def start(self, name, src, dst, device):
        n = len(self.made)
        copy = pltpu.make_async_remote_copy(
            src_ref=src, dst_ref=dst, send_sem=self.send_sem.at[n],
            recv_sem=self.recv_sem.at[n], device_id=device, device_id_type=MESH,
        )
        self.made[name] = copy
        copy.start()

    def arrived(self, name):
        self.made[name].wait_recv()

    def finish(self):
        for copy in self.made.values():
            copy.wait_send()


N_COPIES = 176


def kernel(b_ref, ev_ref, eo_ref, off_ref, out_ref, g_ref, inv_ref, ct_ref, w_ref, evc_ref, amp_ref,
           acc_ref, sb_ref, offb_ref, ry_ref, send_sem, recv_sem, local_sem):
    blk = lax.axis_index("blk")
    rep = lax.axis_index("rep")
    core = lax.rem(blk, 2)
    z = lax.rem(lax.div(blk, 2), NZ)
    x_lo = lax.div(blk, 2 * NZ)
    y = lax.rem(rep, NY)
    x_hi = lax.div(rep, NY)
    x = 2 * x_hi + x_lo
    other = 1 - x_hi

    def device(xx, zz, cc):
        return (lax.rem(xx, 2) * (2 * NZ) + zz * 2 + cc, lax.div(xx, 2) * NY + y)

    x_r, x_l = lax.rem(x + 1, NX), lax.rem(x + NX - 1, NX)
    z_r, z_l = lax.rem(z + 1, NZ), lax.rem(z + NZ - 1, NZ)
    zs = (device(x, z_r, core), device(x, z_l, core))
    xs = (device(x_r, z, core), device(x_l, z, core))
    diagonal = (device(x_r, z_r, core), device(x_l, z_l, core))
    sib = device(x, z, 1 - core)
    peers = []
    for dx in (1, 0):
        for dy in (2, 1, 3, 0):
            if dx or dy:
                to = lax.rem(y + dy, NY)
                xh = other if dx else x_hi
                peers.append((blk, xh * NY + to))

    rows8 = lax.broadcasted_iota(jnp.int32, (8, 128), 0)
    offb_ref[7] = jnp.where(rows8 == 0, off_ref[0], jnp.where(rows8 == 1, off_ref[1], -1))

    barrier = pltpu.get_barrier_semaphore()
    greeted = (*zs, *xs, *diagonal, sib, *peers)
    for who in greeted:
        pl.semaphore_signal(barrier, inc=1, device_id=who, device_id_type=MESH)
    pl.semaphore_wait(barrier, len(greeted))

    copies = Copies(send_sem, recv_sem)
    mine = pl.multiple_of(128 * y + 64 * x_hi, 64)

    def slot(g, par, kind, sgn, c, count=1):
        return g_ref.at[pl.ds(row_of(g, par, kind, sgn, c), PIECE * count), :]

    def same(g, sgn, c, count=1):
        if g == 0:
            return b_ref.at[pl.ds(mine + PIECE * c, PIECE * count), :]
        return slot(g, 0, 0, sgn, c, count)

    def sign(g, d):
        return 0 if g in (0, 4) else d

    def z_send(d, s, c):
        copies.start(("z", d, s, c), same(s, sign(s, d), c), slot(s + 1, 0, 0, sign(s + 1, d), c), zs[d])

    def x_send(g, sgn, c, count=1):
        copies.start(("x", g, sgn, c), same(g, sgn, c, count), slot(g, 0, 1, sgn, c, count), xs[c // 2])

    def sib_send(g, kind, sgn, c, count=1):
        src = same(g, sgn, c, count) if kind == 0 else slot(g, 0, 1, sgn, c, count)
        copies.start(("s", g, kind, sgn, c), src, slot(g, 1, kind, sgn, c, count), sib)

    for i in range(4):
        z_send(0, 0, i)
        z_send(1, 0, 3 - i)
        if i == 0:
            for n, who in enumerate(peers):
                copies.start(("o", n), offb_ref.at[7], offb_ref.at[n], who)
    for c in (0, 2):
        x_send(0, 0, c, 2)
    sib_send(0, 0, 0, 0, 4)
    local = pltpu.make_async_copy(b_ref.at[pl.ds(mine, 64), :], slot(0, 0, 0, 0, 0, 4), local_sem)
    local.start()

    lanes = lax.broadcasted_iota(jnp.int32, (1, 128), 1)
    low = lanes < 64
    ev_y = ev_ref[:, pl.ds(pl.multiple_of(128 * y, 128), 128)]
    ev_swap = jnp.concatenate([ev_y[:, 64:], ev_y[:, :64]], axis=1)
    e_k = eo_ref[blk]
    half_of_lane = lax.div(lanes, 64)
    quarter = lax.rem(lax.div(lanes, 32), 2)
    half_flip = jnp.where(quarter == 0, lax.div(x_l, 2), lax.div(x_r, 2))
    distances = []
    ents = entry_list()
    for n in range(0, 32, 2):
        e_l, dist, half = [], [], []
        for par, kind, dz in ents[n:n + 2]:
            c = core if par == 0 else 1 - core
            xl = x_lo if kind == 0 else 1 - x_lo
            orb = xl * (2 * NZ) + lax.rem(z + dz + NZ, NZ) * 2 + c
            gap = lax.rem(blk - orb + ORBS, ORBS)
            e_l.append(eo_ref[orb])
            dist.append(jnp.minimum(gap, ORBS - gap))
            half.append(jnp.full((1, 128), x_hi, jnp.int32) if kind == 0 else half_flip)
        want = jnp.where(low, half[0], half[1])
        ev_b = jnp.where(want == half_of_lane, ev_y, ev_swap)
        ct_ref[:, 64 * n:64 * n + 128] = ev_b - e_k - jnp.where(low, e_l[0], e_l[1])
        distances.append((64 * n, jnp.where(low, dist[0], dist[1])))
    for n in range(4):
        tile = jnp.broadcast_to(ev_ref[:, 128 * n:128 * n + 128], (128, 128))
        evc_ref[128 * n:128 * n + 128, :] = tile.T

    def invert(i, carry):
        rows = pl.ds(pl.multiple_of(i * 32, 32), 32)
        ev_a = evc_ref[rows, :]
        for n in range(16):
            cols = slice(128 * n, 128 * n + 128)
            inv_ref[rows, cols] = -1.0 / (ev_a + ct_ref[:, cols])
        return carry

    lax.fori_loop(0, 16, invert, 0)

    def weigh():
        for n in range(7):
            copies.arrived(("o", n))
        table = offb_ref[...].reshape(64, 128)
        for col, dist in distances:
            count = jnp.sum(jnp.where(table == dist, 1.0, 0.0), axis=0, keepdims=True)
            w_ref[:, col:col + 128] = jnp.where(dist == 0, 2.0 * count, count)

    def amplitudes(n):
        cols = slice(BLOCK * n, BLOCK * n + BLOCK)
        right = g_ref[cols, :]
        weight = w_ref[:, cols]
        for m in range(2):
            rows = slice(256 * m, 256 * m + 256)
            pair = lax.dot_general(b_ref[rows, :], right, (((1,), (1,)), ((), ())),
                                   preferred_element_type=F32)
            amp_ref[n % 2, rows, :] = (pair * (inv_ref[rows, cols] * weight)).astype(BF16)

    def contract(n):
        for m in range(4):
            res = jnp.dot(amp_ref[n % 2], g_ref[BLOCK * n:BLOCK * n + BLOCK, 256 * m:256 * m + 256],
                          preferred_element_type=F32)
            for h in range(2):
                val = res[:, 128 * h:128 * h + 128]
                if n > 0:
                    val = val + acc_ref[2 * m + h]
                acc_ref[2 * m + h] = val

    def contract_last(which, rows):
        for m in range(2):
            cols = pl.ds(pl.multiple_of(which * 512 + 256 * m, 256), 256)
            res = jnp.dot(amp_ref[1, rows, :], g_ref[7 * BLOCK:, cols], preferred_element_type=F32)
            for h in range(2):
                j = which * NY + 2 * m + h
                val = res[:, 128 * h:128 * h + 128] + acc_ref[j, rows, :]
                acc_ref[j, rows, :] = val
                sb_ref[j, rows, :] = val.astype(BF16)

    def sib_arrived(g, kind):
        for sgn in range(1 if g in (0, 4) else 2):
            if g == 0 and kind == 0:
                copies.arrived(("s", 0, 0, 0, 0))
            elif g == 4:
                for c in range(4):
                    copies.arrived(("s", g, kind, 0, c))
            else:
                for c in (0, 2):
                    copies.arrived(("s", g, kind, sgn, c))

    def x_arrivals(g, i):
        if g == 0:
            for c in (0, 2):
                copies.arrived(("x", 0, 0, c))
                sib_send(0, 1, 0, c, 2)
            return
        for d, c in ((0, i), (1, 3 - i)):
            copies.arrived(("x", g, d, c))
            if i % 2 == 1:
                sib_send(g, 1, d, c // 2 * 2, 2)

    for s in range(1, 5):
        for i in range(4 if s < 4 else 2):
            for d, c in ((0, i), (1, 3 - i)):
                copies.arrived(("z", d, s - 1, c))
                if s < 3 or (s == 3 and i < 2):
                    z_send(d, s, c)
                if s == 3 and i < 2:
                    copies.start(("d", d, c), slot(3, 0, 0, d, c), slot(4, 0, 1, 0, c), diagonal[d])
            for d, c in ((0, i), (1, 3 - i)):
                if s < 4:
                    x_send(s, d, c)
                    if i % 2 == 1:
                        sib_send(s, 0, d, c // 2 * 2, 2)
                else:
                    sib_send(4, 0, 0, c)
            if s == 1 and i == 1:
                x_arrivals(0, 0)
            if s > 1:
                if i > 0:
                    x_arrivals(s - 1, i - 1)
            if i == 3 and s > 1:
                x_arrivals(s - 1, 3)
            if (s, i) == (1, 3):
                weigh()
                sib_arrived(0, 0)
                sib_arrived(0, 1)
                local.wait()
                amplitudes(0)
                contract(0)
            if (s, i) == (2, 1):
                sib_arrived(1, 0)
                amplitudes(1)
            if (s, i) == (2, 2):
                contract(1)
            if (s, i) == (3, 1):
                sib_arrived(1, 1)
                amplitudes(2)
            if (s, i) == (3, 2):
                contract(2)
                sib_arrived(2, 0)
                amplitudes(3)
            if (s, i) == (3, 3):
                contract(3)
            if (s, i) == (4, 0):
                sib_arrived(2, 1)
                amplitudes(4)
            if (s, i) == (4, 1):
                for d, c in ((0, 0), (1, 3), (0, 1), (1, 2)):
                    copies.arrived(("d", d, c))
                    sib_send(4, 1, 0, c)
                for j in (1, 2, 3):
                    x_arrivals(3, j)
                contract(4)
                sib_arrived(3, 0)
                amplitudes(5)
                contract(5)
    sib_arrived(3, 1)
    amplitudes(6)
    contract(6)
    sib_arrived(4, 0)
    sib_arrived(4, 1)
    amplitudes(7)

    halves = (slice(0, 256), slice(256, 512))
    for k, which in enumerate((other, x_hi)):
        for m, rows in enumerate(halves):
            contract_last(which, rows)
            for n, who in enumerate(peers):
                if (n < 4) == (k == 0):
                    part = pl.ds(256 * m, 256)
                    copies.start(("r", n, m), sb_ref.at[who[1], part, :], ry_ref.at[n, part, :], who)
    for m, rows in enumerate(halves):
        total = acc_ref[rep, rows, :]
        for n in range(7):
            copies.arrived(("r", n, m))
            total = total + ry_ref[n, rows, :].astype(F32)
        out_ref[0, rows, :] = total
    copies.finish()


def per_device(integrals, eps_occ, eps_vir, offsets):
    v, aux = integrals.shape[1:]
    vmem = pl.BlockSpec(memory_space=pltpu.VMEM)
    smem = pl.BlockSpec(memory_space=pltpu.SMEM)
    return pl.pallas_call(
        kernel,
        out_shape=jax.ShapeDtypeStruct((1, v, aux // 8), F32),
        in_specs=[vmem, vmem, smem, smem],
        out_specs=vmem,
        scratch_shapes=[
            pltpu.VMEM((2048, aux), BF16),
            pltpu.VMEM((v, 2048), F32),
            pltpu.VMEM((1, 2048), F32),
            pltpu.VMEM((1, 2048), F32),
            pltpu.VMEM((v, 128), F32),
            pltpu.VMEM((2, v, BLOCK), BF16),
            pltpu.VMEM((8, v, 128), F32),
            pltpu.VMEM((8, v, 128), BF16),
            pltpu.VMEM((8, 8, 128), jnp.int32),
            pltpu.VMEM((7, v, 128), BF16),
            pltpu.SemaphoreType.DMA((N_COPIES,)),
            pltpu.SemaphoreType.DMA((N_COPIES,)),
            pltpu.SemaphoreType.DMA,
        ],
        compiler_params=pltpu.CompilerParams(
            collective_id=0, has_side_effects=True, vmem_limit_bytes=56 << 20
        ),
        name="pair_amplitudes",
    )(integrals[0], eps_vir[None, :], eps_occ, offsets)


def solution(mesh):
    in_specs = (P("blk", None, None), P(), P(), P("rep"))
    out_specs = P("blk", None, "rep")
    return jax.shard_map(
        per_device, mesh=mesh, in_specs=in_specs, out_specs=out_specs, check_vma=False
    )
```

```python
import jax
import jax.numpy as jnp
from jax import lax
from jax.experimental import pallas as pl
from jax.experimental.pallas import tpu as pltpu
from jax.sharding import PartitionSpec as P

MESH = pl.DeviceIdType.MESH
F32 = jnp.float32
BF16 = jnp.bfloat16

NZ, NY, NX = 8, 4, 4
ORBS = 32
PIECE = 16
BLOCK = 256
X_FIRST, Y_FIRST, DIRECT = slice(0, 192), slice(192, 384), slice(384, 512)


def row_of(g, par, kind, sgn, c):
    if g in (0, 4):
        entry = (0 if g == 0 else 28) + kind * 2 + par
    else:
        entry = 4 + (g - 1) * 8 + kind * 4 + par * 2 + sgn
    return entry * 64 + PIECE * c


def entry_list():
    out = [None] * 32
    for g in range(5):
        for par in range(2):
            for kind in range(2):
                for sgn in range(1 if g in (0, 4) else 2):
                    out[row_of(g, par, kind, sgn, 0) // 64] = (par, kind, g if sgn else -g)
    return out


class Copies:
    def __init__(self, send_sem, recv_sem):
        self.send_sem, self.recv_sem = send_sem, recv_sem
        self.made = {}

    def start(self, name, src, dst, device):
        n = len(self.made)
        copy = pltpu.make_async_remote_copy(
            src_ref=src, dst_ref=dst, send_sem=self.send_sem.at[n],
            recv_sem=self.recv_sem.at[n], device_id=device, device_id_type=MESH,
        )
        self.made[name] = copy
        copy.start()

    def arrived(self, name):
        self.made[name].wait_recv()

    def finish(self):
        for copy in self.made.values():
            copy.wait_send()


N_COPIES = 176


def kernel(b_ref, ev_ref, eo_ref, off_ref, out_ref, g_ref, inv_ref, ct_ref, w_ref, evc_ref, amp_ref,
           acc_ref, sb_ref, offb_ref, rd_ref, rx_ref, ry_ref, t3_ref, ry2_ref, t2_ref, rx2_ref, send_sem, recv_sem, local_sem):
    blk = lax.axis_index("blk")
    rep = lax.axis_index("rep")
    core = lax.rem(blk, 2)
    z = lax.rem(lax.div(blk, 2), NZ)
    x_lo = lax.div(blk, 2 * NZ)
    y = lax.rem(rep, NY)
    x_hi = lax.div(rep, NY)
    x = 2 * x_hi + x_lo
    other = 1 - x_hi

    def device(xx, zz, cc):
        return (lax.rem(xx, 2) * (2 * NZ) + zz * 2 + cc, lax.div(xx, 2) * NY + y)

    x_r, x_l = lax.rem(x + 1, NX), lax.rem(x + NX - 1, NX)
    z_r, z_l = lax.rem(z + 1, NZ), lax.rem(z + NZ - 1, NZ)
    zs = (device(x, z_r, core), device(x, z_l, core))
    xs = (device(x_r, z, core), device(x_l, z, core))
    diagonal = (device(x_r, z_r, core), device(x_l, z_l, core))
    sib = device(x, z, 1 - core)
    y_r, y_l, y_o = lax.rem(y + 1, NY), lax.rem(y + NY - 1, NY), lax.rem(y + 2, NY)
    ys = ((blk, x_hi * NY + y_r), (blk, x_hi * NY + y_l), (blk, x_hi * NY + y_o))
    partner = (blk, other * NY + y)
    peers = []
    for dx in (1, 0):
        for dy in (2, 1, 3, 0):
            if dx or dy:
                to = lax.rem(y + dy, NY)
                xh = other if dx else x_hi
                peers.append((blk, xh * NY + to))

    rows8 = lax.broadcasted_iota(jnp.int32, (8, 128), 0)
    offb_ref[0] = jnp.where(rows8 == 0, off_ref[0], jnp.where(rows8 == 1, off_ref[1], -1))

    barrier = pltpu.get_barrier_semaphore()
    greeted = (*zs, *xs, *ys[:2], sib)
    for who in greeted:
        pl.semaphore_signal(barrier, inc=1, device_id=who, device_id_type=MESH)
    pl.semaphore_wait(barrier, len(greeted))

    copies = Copies(send_sem, recv_sem)
    mine = pl.multiple_of(128 * y + 64 * x_hi, 64)

    def slot(g, par, kind, sgn, c, count=1):
        return g_ref.at[pl.ds(row_of(g, par, kind, sgn, c), PIECE * count), :]

    def same(g, sgn, c, count=1):
        if g == 0:
            return b_ref.at[pl.ds(mine + PIECE * c, PIECE * count), :]
        return slot(g, 0, 0, sgn, c, count)

    def sign(g, d):
        return 0 if g in (0, 4) else d

    def z_send(d, s, c):
        copies.start(("z", d, s, c), same(s, sign(s, d), c), slot(s + 1, 0, 0, sign(s + 1, d), c), zs[d])

    def x_send(g, sgn, c, count=1):
        copies.start(("x", g, sgn, c), same(g, sgn, c, count), slot(g, 0, 1, sgn, c, count), xs[c // 2])

    def sib_send(g, kind, sgn, c, count=1):
        src = same(g, sgn, c, count) if kind == 0 else slot(g, 0, 1, sgn, c, count)
        copies.start(("s", g, kind, sgn, c), src, slot(g, 1, kind, sgn, c, count), sib)

    for i in range(4):
        z_send(0, 0, i)
        z_send(1, 0, 3 - i)
        if i == 0:
            for n in range(2):
                copies.start(("o", n), offb_ref.at[0], offb_ref.at[1 + n], ys[n])
    for c in (0, 2):
        x_send(0, 0, c, 2)
    sib_send(0, 0, 0, 0, 4)
    local = pltpu.make_async_copy(b_ref.at[pl.ds(mine, 64), :], slot(0, 0, 0, 0, 0, 4), local_sem)
    local.start()

    lanes = lax.broadcasted_iota(jnp.int32, (1, 128), 1)
    low = lanes < 64
    ev_y = ev_ref[:, pl.ds(pl.multiple_of(128 * y, 128), 128)]
    ev_swap = jnp.concatenate([ev_y[:, 64:], ev_y[:, :64]], axis=1)
    e_k = eo_ref[blk]
    half_of_lane = lax.div(lanes, 64)
    quarter = lax.rem(lax.div(lanes, 32), 2)
    half_flip = jnp.where(quarter == 0, lax.div(x_l, 2), lax.div(x_r, 2))
    distances = []
    ents = entry_list()
    for n in range(0, 32, 2):
        e_l, dist, half = [], [], []
        for par, kind, dz in ents[n:n + 2]:
            c = core if par == 0 else 1 - core
            xl = x_lo if kind == 0 else 1 - x_lo
            orb = xl * (2 * NZ) + lax.rem(z + dz + NZ, NZ) * 2 + c
            gap = lax.rem(blk - orb + ORBS, ORBS)
            e_l.append(eo_ref[orb])
            dist.append(jnp.minimum(gap, ORBS - gap))
            half.append(jnp.full((1, 128), x_hi, jnp.int32) if kind == 0 else half_flip)
        want = jnp.where(low, half[0], half[1])
        ev_b = jnp.where(want == half_of_lane, ev_y, ev_swap)
        ct_ref[:, 64 * n:64 * n + 128] = ev_b - e_k - jnp.where(low, e_l[0], e_l[1])
        distances.append((64 * n, jnp.where(low, dist[0], dist[1])))
    for n in range(4):
        tile = jnp.broadcast_to(ev_ref[:, 128 * n:128 * n + 128], (128, 128))
        evc_ref[128 * n:128 * n + 128, :] = tile.T

    def invert(i, carry):
        rows = pl.ds(pl.multiple_of(i * 32, 32), 32)
        ev_a = evc_ref[rows, :]
        for n in range(16):
            cols = slice(128 * n, 128 * n + 128)
            inv_ref[rows, cols] = -1.0 / (ev_a + ct_ref[:, cols])
        return carry

    lax.fori_loop(0, 16, invert, 0)

    def weigh():
        copies.arrived(("o", 3))
        table = offb_ref[...].reshape(64, 128)
        for col, dist in distances:
            count = jnp.sum(jnp.where(table == dist, 1.0, 0.0), axis=0, keepdims=True)
            w_ref[:, col:col + 128] = jnp.where(dist == 0, 2.0 * count, count)

    def amplitudes(n):
        cols = slice(BLOCK * n, BLOCK * n + BLOCK)
        right = g_ref[cols, :]
        weight = w_ref[:, cols]
        for m in range(2):
            rows = slice(256 * m, 256 * m + 256)
            pair = lax.dot_general(b_ref[rows, :], right, (((1,), (1,)), ((), ())),
                                   preferred_element_type=F32)
            amp_ref[n % 2, rows, :] = (pair * (inv_ref[rows, cols] * weight)).astype(BF16)

    def contract(n):
        for m in range(4):
            res = jnp.dot(amp_ref[n % 2], g_ref[BLOCK * n:BLOCK * n + BLOCK, 256 * m:256 * m + 256],
                          preferred_element_type=F32)
            for h in range(2):
                val = res[:, 128 * h:128 * h + 128]
                if n > 0:
                    val = val + acc_ref[2 * m + h]
                acc_ref[2 * m + h] = val

    def contract_last(which, rows):
        for m in range(2):
            cols = pl.ds(pl.multiple_of(which * 512 + 256 * m, 256), 256)
            res = jnp.dot(amp_ref[1, rows, :], g_ref[7 * BLOCK:, cols], preferred_element_type=F32)
            for h in range(2):
                j = which * NY + 2 * m + h
                val = res[:, 128 * h:128 * h + 128] + acc_ref[j, rows, :]
                acc_ref[j, rows, :] = val
                sb_ref[j, rows, :] = val.astype(BF16)

    def sib_arrived(g, kind):
        for sgn in range(1 if g in (0, 4) else 2):
            if g == 0 and kind == 0:
                copies.arrived(("s", 0, 0, 0, 0))
            elif g == 4:
                for c in range(4):
                    copies.arrived(("s", g, kind, 0, c))
            else:
                for c in (0, 2):
                    copies.arrived(("s", g, kind, sgn, c))

    def x_arrivals(g, i):
        if g == 0:
            for c in (0, 2):
                copies.arrived(("x", 0, 0, c))
                sib_send(0, 1, 0, c, 2)
            return
        for d, c in ((0, i), (1, 3 - i)):
            copies.arrived(("x", g, d, c))
            if i % 2 == 1:
                sib_send(g, 1, d, c // 2 * 2, 2)

    for s in range(1, 5):
        for i in range(4 if s < 4 else 2):
            for d, c in ((0, i), (1, 3 - i)):
                copies.arrived(("z", d, s - 1, c))
                if s < 3 or (s == 3 and i < 2):
                    z_send(d, s, c)
                if s == 3 and i < 2:
                    copies.start(("d", d, c), slot(3, 0, 0, d, c), slot(4, 0, 1, 0, c), diagonal[d])
            for d, c in ((0, i), (1, 3 - i)):
                if s < 4:
                    x_send(s, d, c)
                    if i % 2 == 1:
                        sib_send(s, 0, d, c // 2 * 2, 2)
                else:
                    sib_send(4, 0, 0, c)
            if s == 1 and i == 1:
                x_arrivals(0, 0)
            if s > 1:
                if i > 0:
                    x_arrivals(s - 1, i - 1)
            if i == 3 and s > 1:
                x_arrivals(s - 1, 3)
            if (s, i) == (1, 0):
                copies.arrived(("o", 0))
                copies.start(("o", 2), offb_ref.at[1], offb_ref.at[3], ys[0])
            if (s, i) == (2, 0):
                copies.arrived(("o", 1))
                copies.arrived(("o", 2))
                copies.start(("o", 3), offb_ref.at[pl.ds(0, 4)], offb_ref.at[pl.ds(4, 4)], partner)
            if (s, i) == (2, 2):
                sib_arrived(0, 0)
                sib_arrived(0, 1)
                local.wait()
                weigh()
                amplitudes(0)
                contract(0)
            if (s, i) == (2, 3):
                sib_arrived(1, 0)
                amplitudes(1)
            if (s, i) == (3, 0):
                contract(1)
            if (s, i) == (3, 1):
                sib_arrived(1, 1)
                amplitudes(2)
                contract(2)
            if (s, i) == (3, 2):
                sib_arrived(2, 0)
                amplitudes(3)
            if (s, i) == (3, 3):
                contract(3)
            if (s, i) == (4, 0):
                sib_arrived(2, 1)
                amplitudes(4)
            if (s, i) == (4, 1):
                for d, c in ((0, 0), (1, 3), (0, 1), (1, 2)):
                    copies.arrived(("d", d, c))
                    sib_send(4, 1, 0, c)
                for j in (1, 2, 3):
                    x_arrivals(3, j)
                contract(4)
                sib_arrived(3, 0)
                amplitudes(5)
                contract(5)
    sib_arrived(3, 1)
    amplitudes(6)
    contract(6)
    sib_arrived(4, 0)
    sib_arrived(4, 1)
    amplitudes(7)

    def sliced(ref, which, to, rows):
        return ref.at[which * NY + to, pl.ds(rows.start, rows.stop - rows.start), :]

    contract_last(other, X_FIRST)
    copies.start(("x1", 0), sb_ref.at[pl.ds(other * NY, NY), pl.ds(0, 192), :], rx_ref, partner)
    for which in (0, 1):
        contract_last(which, Y_FIRST)
        for n, to in enumerate((y_r, y_l, y_o)):
            copies.start(("y1", n, which), sliced(sb_ref, which, to, Y_FIRST), ry_ref.at[n, which], ys[n])
    for which in (0, 1):
        contract_last(which, DIRECT)
    for n, who in enumerate(peers):
        copies.start(("r", n), sb_ref.at[who[1], pl.ds(384, 128), :], rd_ref.at[n], who)
    contract_last(x_hi, X_FIRST)

    copies.arrived(("x1", 0))
    for to in range(NY):
        t3_ref[to] = (acc_ref[x_hi * NY + to, X_FIRST, :] + rx_ref[to].astype(F32)).astype(BF16)
    for n, to in enumerate((y_r, y_l, y_o)):
        copies.start(("y2", n), t3_ref.at[to], ry2_ref.at[n], ys[n])

    def y_sum(which):
        total = acc_ref[which * NY + y, Y_FIRST, :]
        for n in range(3):
            total = total + ry_ref[n, which].astype(F32)
        return total

    for n in range(3):
        for which in (0, 1):
            copies.arrived(("y1", n, which))
    t2_ref[...] = y_sum(other).astype(BF16)
    copies.start(("x2", 0), t2_ref, rx2_ref, partner)
    total = acc_ref[rep, DIRECT, :]
    for n in range(7):
        copies.arrived(("r", n))
        total = total + rd_ref[n].astype(F32)
    out_ref[0, DIRECT, :] = total
    total = acc_ref[rep, X_FIRST, :] + rx_ref[y].astype(F32)
    for n in range(3):
        copies.arrived(("y2", n))
        total = total + ry2_ref[n].astype(F32)
    out_ref[0, X_FIRST, :] = total
    total = y_sum(x_hi)
    copies.arrived(("x2", 0))
    out_ref[0, Y_FIRST, :] = total + rx2_ref[...].astype(F32)
    copies.finish()


def per_device(integrals, eps_occ, eps_vir, offsets):
    v, aux = integrals.shape[1:]
    n_x, n_y, n_d = (part.stop - part.start for part in (X_FIRST, Y_FIRST, DIRECT))
    vmem = pl.BlockSpec(memory_space=pltpu.VMEM)
    smem = pl.BlockSpec(memory_space=pltpu.SMEM)
    return pl.pallas_call(
        kernel,
        out_shape=jax.ShapeDtypeStruct((1, v, aux // 8), F32),
        in_specs=[vmem, vmem, smem, smem],
        out_specs=vmem,
        scratch_shapes=[
            pltpu.VMEM((2048, aux), BF16),
            pltpu.VMEM((v, 2048), F32),
            pltpu.VMEM((1, 2048), F32),
            pltpu.VMEM((1, 2048), F32),
            pltpu.VMEM((v, 128), F32),
            pltpu.VMEM((2, v, BLOCK), BF16),
            pltpu.VMEM((8, v, 128), F32),
            pltpu.VMEM((8, v, 128), BF16),
            pltpu.VMEM((8, 8, 128), jnp.int32),
            pltpu.VMEM((7, n_d, 128), BF16),
            pltpu.VMEM((NY, n_x, 128), BF16),
            pltpu.VMEM((3, 2, n_y, 128), BF16),
            pltpu.VMEM((NY, n_x, 128), BF16),
            pltpu.VMEM((3, n_x, 128), BF16),
            pltpu.VMEM((n_y, 128), BF16),
            pltpu.VMEM((n_y, 128), BF16),
            pltpu.SemaphoreType.DMA((N_COPIES,)),
            pltpu.SemaphoreType.DMA((N_COPIES,)),
            pltpu.SemaphoreType.DMA,
        ],
        compiler_params=pltpu.CompilerParams(
            collective_id=0, has_side_effects=True, vmem_limit_bytes=56 << 20
        ),
        name="pair_amplitudes",
    )(integrals[0], eps_vir[None, :], eps_occ, offsets)


def solution(mesh):
    in_specs = (P("blk", None, None), P(), P(), P("rep"))
    out_specs = P("blk", None, "rep")
    return jax.shard_map(
        per_device, mesh=mesh, in_specs=in_specs, out_specs=out_specs, check_vma=False
    )
```

```python
import jax
import jax.numpy as jnp
from jax import lax
from jax.experimental import pallas as pl
from jax.experimental.pallas import tpu as pltpu
from jax.sharding import PartitionSpec as P

MESH = pl.DeviceIdType.MESH
F32 = jnp.float32
BF16 = jnp.bfloat16

NZ, NY, NX = 8, 4, 4
ORBS = 32
PIECE = 16
BLOCK = 256
X_FIRST, Y_FIRST, DIRECT = slice(0, 192), slice(192, 384), slice(384, 512)


def row_of(g, par, kind, sgn, c):
    if g == 0:
        entry = kind * 2 + par
    elif g == 4:
        entry = 24 + par * 4 + 2 + kind
    elif g == 3 and kind == 1:
        entry = 24 + par * 4 + sgn
    else:
        entry = 4 + (g - 1) * 8 + kind * 4 + par * 2 + sgn
    return entry * 64 + PIECE * c


def entry_list():
    out = [None] * 32
    for g in range(5):
        for par in range(2):
            for kind in range(2):
                for sgn in range(1 if g in (0, 4) else 2):
                    out[row_of(g, par, kind, sgn, 0) // 64] = (par, kind, g if sgn else -g)
    return out


class Copies:
    def __init__(self, send_sem, recv_sem):
        self.send_sem, self.recv_sem = send_sem, recv_sem
        self.made = {}

    def start(self, name, src, dst, device):
        n = len(self.made)
        copy = pltpu.make_async_remote_copy(
            src_ref=src, dst_ref=dst, send_sem=self.send_sem.at[n],
            recv_sem=self.recv_sem.at[n], device_id=device, device_id_type=MESH,
        )
        self.made[name] = copy
        copy.start()

    def arrived(self, name):
        self.made[name].wait_recv()

    def finish(self):
        for copy in self.made.values():
            copy.wait_send()


N_COPIES = 176


def kernel(b_hbm, ev_hbm, eo_hbm, off_hbm, out_hbm, b_ref, ev_ref, eo_ref, off_ref, out_ref, g_ref, inv_ref, ct_ref, w_ref, evc_ref, amp_ref,
           acc_ref, sb_ref, offb_ref, rd_ref, rx_ref, ry_ref, t3_ref, ry2_ref, t2_ref, rx2_ref, send_sem, recv_sem, local_sem):
    blk = lax.axis_index("blk")
    rep = lax.axis_index("rep")
    core = lax.rem(blk, 2)
    z = lax.rem(lax.div(blk, 2), NZ)
    x_lo = lax.div(blk, 2 * NZ)
    y = lax.rem(rep, NY)
    x_hi = lax.div(rep, NY)
    x = 2 * x_hi + x_lo
    other = 1 - x_hi

    def device(xx, zz, cc):
        return (lax.rem(xx, 2) * (2 * NZ) + zz * 2 + cc, lax.div(xx, 2) * NY + y)

    x_r, x_l = lax.rem(x + 1, NX), lax.rem(x + NX - 1, NX)
    z_r, z_l = lax.rem(z + 1, NZ), lax.rem(z + NZ - 1, NZ)
    zs = (device(x, z_r, core), device(x, z_l, core))
    xs = (device(x_r, z, core), device(x_l, z, core))
    diagonal = (device(x_r, z_r, core), device(x_l, z_l, core))
    sib = device(x, z, 1 - core)
    y_r, y_l, y_o = lax.rem(y + 1, NY), lax.rem(y + NY - 1, NY), lax.rem(y + 2, NY)
    ys = ((blk, x_hi * NY + y_r), (blk, x_hi * NY + y_l), (blk, x_hi * NY + y_o))
    partner = (blk, other * NY + y)
    peers = []
    for dx in (1, 0):
        for dy in (2, 1, 3, 0):
            if dx or dy:
                to = lax.rem(y + dy, NY)
                xh = other if dx else x_hi
                peers.append((blk, xh * NY + to))

    loads = []
    for n, (src, dst) in enumerate(((off_hbm, off_ref), (b_hbm, b_ref), (ev_hbm, ev_ref), (eo_hbm, eo_ref))):
        loads.append(pltpu.make_async_copy(src, dst, local_sem.at[1 + n]))

    barrier = pltpu.get_barrier_semaphore()
    greeted = (*zs, *xs, *ys[:2], sib)
    for who in greeted:
        pl.semaphore_signal(barrier, inc=1, device_id=who, device_id_type=MESH)
    for load in loads:
        load.start()
    loads[0].wait()
    rows8 = lax.broadcasted_iota(jnp.int32, (8, 128), 0)
    offb_ref[0] = jnp.where(rows8 == 0, off_ref[0], jnp.where(rows8 == 1, off_ref[1], -1))
    loads[1].wait()
    pl.semaphore_wait(barrier, len(greeted))

    copies = Copies(send_sem, recv_sem)
    mine = pl.multiple_of(128 * y + 64 * x_hi, 64)

    def slot(g, par, kind, sgn, c, count=1):
        return g_ref.at[pl.ds(row_of(g, par, kind, sgn, c), PIECE * count), :]

    def same(g, sgn, c, count=1):
        if g == 0:
            return b_ref.at[pl.ds(mine + PIECE * c, PIECE * count), :]
        return slot(g, 0, 0, sgn, c, count)

    def sign(g, d):
        return 0 if g in (0, 4) else d

    def z_send(d, s, c):
        copies.start(("z", d, s, c), same(s, sign(s, d), c), slot(s + 1, 0, 0, sign(s + 1, d), c), zs[d])

    def x_send(g, sgn, c, count=1):
        copies.start(("x", g, sgn, c), same(g, sgn, c, count), slot(g, 0, 1, sgn, c, count), xs[c // 2])

    def sib_send(g, kind, sgn, c, count=1):
        src = same(g, sgn, c, count) if kind == 0 else slot(g, 0, 1, sgn, c, count)
        copies.start(("s", g, kind, sgn, c), src, slot(g, 1, kind, sgn, c, count), sib)

    for n in range(2):
        copies.start(("o", n), offb_ref.at[0], offb_ref.at[1 + n], ys[n])
    for i in range(4):
        z_send(0, 0, i)
        z_send(1, 0, 3 - i)
    for c in (0, 2):
        x_send(0, 0, c, 2)
    sib_send(0, 0, 0, 0, 4)
    local = pltpu.make_async_copy(b_ref.at[pl.ds(mine, 64), :], slot(0, 0, 0, 0, 0, 4), local_sem.at[0])
    local.start()

    loads[2].wait()
    loads[3].wait()
    lanes = lax.broadcasted_iota(jnp.int32, (1, 128), 1)
    low = lanes < 64
    ev_y = ev_ref[:, pl.ds(pl.multiple_of(128 * y, 128), 128)]
    ev_swap = jnp.concatenate([ev_y[:, 64:], ev_y[:, :64]], axis=1)
    e_k = eo_ref[blk]
    half_of_lane = lax.div(lanes, 64)
    quarter = lax.rem(lax.div(lanes, 32), 2)
    half_flip = jnp.where(quarter == 0, lax.div(x_l, 2), lax.div(x_r, 2))
    distances = []
    ents = entry_list()
    for n in range(0, 32, 2):
        e_l, dist, half = [], [], []
        for par, kind, dz in ents[n:n + 2]:
            c = core if par == 0 else 1 - core
            xl = x_lo if kind == 0 else 1 - x_lo
            orb = xl * (2 * NZ) + lax.rem(z + dz + NZ, NZ) * 2 + c
            gap = lax.rem(blk - orb + ORBS, ORBS)
            e_l.append(eo_ref[orb])
            dist.append(jnp.minimum(gap, ORBS - gap))
            half.append(jnp.full((1, 128), x_hi, jnp.int32) if kind == 0 else half_flip)
        want = jnp.where(low, half[0], half[1])
        ev_b = jnp.where(want == half_of_lane, ev_y, ev_swap)
        ct_ref[:, 64 * n:64 * n + 128] = ev_b - e_k - jnp.where(low, e_l[0], e_l[1])
        distances.append((64 * n, jnp.where(low, dist[0], dist[1])))
    for n in range(4):
        tile = jnp.broadcast_to(ev_ref[:, 128 * n:128 * n + 128], (128, 128))
        evc_ref[128 * n:128 * n + 128, :] = tile.T

    def invert(i, carry):
        rows = pl.ds(pl.multiple_of(i * 32, 32), 32)
        ev_a = evc_ref[rows, :]
        for n in range(16):
            cols = slice(128 * n, 128 * n + 128)
            inv_ref[rows, cols] = -1.0 / (ev_a + ct_ref[:, cols])
        return carry

    lax.fori_loop(0, 16, invert, 0)

    def weigh():
        copies.arrived(("o", 3))
        table = offb_ref[...].reshape(64, 128)
        for col, dist in distances:
            count = jnp.sum(jnp.where(table == dist, 1.0, 0.0), axis=0, keepdims=True)
            w_ref[:, col:col + 128] = jnp.where(dist == 0, 2.0 * count, count)

    def amplitudes(n):
        cols = slice(BLOCK * n, BLOCK * n + BLOCK)
        right = g_ref[cols, :]
        weight = w_ref[:, cols]
        for m in range(2):
            rows = slice(256 * m, 256 * m + 256)
            pair = lax.dot_general(b_ref[rows, :], right, (((1,), (1,)), ((), ())),
                                   preferred_element_type=F32)
            amp_ref[n % 2, rows, :] = (pair * (inv_ref[rows, cols] * weight)).astype(BF16)

    def products(n):
        cols = slice(BLOCK * n, BLOCK * n + BLOCK)
        right = g_ref[cols, :]
        for m in range(2):
            rows = slice(256 * m, 256 * m + 256)
            pair = lax.dot_general(b_ref[rows, :], right, (((1,), (1,)), ((), ())),
                                   preferred_element_type=F32)
            inv_ref[rows, cols] = pair * inv_ref[rows, cols]

    def weighted(n):
        cols = slice(BLOCK * n, BLOCK * n + BLOCK)
        amp_ref[n % 2] = (inv_ref[:, cols] * w_ref[:, cols]).astype(BF16)

    def contract(n):
        for m in range(4):
            res = jnp.dot(amp_ref[n % 2], g_ref[BLOCK * n:BLOCK * n + BLOCK, 256 * m:256 * m + 256],
                          preferred_element_type=F32)
            for h in range(2):
                val = res[:, 128 * h:128 * h + 128]
                if n > 0:
                    val = val + acc_ref[2 * m + h]
                acc_ref[2 * m + h] = val

    def contract_last(which, rows):
        for m in range(2):
            cols = pl.ds(pl.multiple_of(which * 512 + 256 * m, 256), 256)
            res = jnp.dot(amp_ref[1, rows, :], g_ref[7 * BLOCK:, cols], preferred_element_type=F32)
            for h in range(2):
                j = which * NY + 2 * m + h
                val = res[:, 128 * h:128 * h + 128] + acc_ref[j, rows, :]
                acc_ref[j, rows, :] = val
                sb_ref[j, rows, :] = val.astype(BF16)

    def sib_arrived(g, kind):
        for sgn in range(1 if g in (0, 4) else 2):
            if g == 0 and kind == 0:
                copies.arrived(("s", 0, 0, 0, 0))
            elif g == 4:
                for c in range(4):
                    copies.arrived(("s", g, kind, 0, c))
            else:
                for c in (0, 2):
                    copies.arrived(("s", g, kind, sgn, c))

    def x_arrivals(g, i):
        if g == 0:
            for c in (0, 2):
                copies.arrived(("x", 0, 0, c))
                sib_send(0, 1, 0, c, 2)
            return
        for d, c in ((0, i), (1, 3 - i)):
            copies.arrived(("x", g, d, c))
            if i % 2 == 1:
                sib_send(g, 1, d, c // 2 * 2, 2)

    copies.arrived(("o", 0))
    copies.start(("o", 2), offb_ref.at[1], offb_ref.at[3], ys[0])
    for s in range(1, 5):
        for i in range(4 if s < 4 else 2):
            for d, c in ((0, i), (1, 3 - i)):
                copies.arrived(("z", d, s - 1, c))
                if s < 3 or (s == 3 and i < 2):
                    z_send(d, s, c)
                if s == 3 and i < 2:
                    copies.start(("d", d, c), slot(3, 0, 0, d, c), slot(4, 0, 1, 0, c), diagonal[d])
            for d, c in ((0, i), (1, 3 - i)):
                if s < 4:
                    x_send(s, d, c)
                    if i % 2 == 1:
                        sib_send(s, 0, d, c // 2 * 2, 2)
                else:
                    sib_send(4, 0, 0, c)
            if s == 1 and i == 1:
                x_arrivals(0, 0)
            if s in (2, 3) and i > 0:
                x_arrivals(s - 1, i - 1)
            if s in (2, 3) and i == 3:
                x_arrivals(s - 1, 3)
            if (s, i) == (4, 0):
                x_arrivals(3, 0)
                x_arrivals(3, 1)
            if (s, i) == (4, 1):
                x_arrivals(3, 2)
                x_arrivals(3, 3)
            if (s, i) == (1, 3):
                copies.arrived(("o", 1))
                copies.arrived(("o", 2))
                copies.start(("o", 3), offb_ref.at[pl.ds(0, 4)], offb_ref.at[pl.ds(4, 4)], partner)
            if (s, i) == (2, 0):
                sib_arrived(0, 0)
                sib_arrived(0, 1)
                local.wait()
                products(0)
            if (s, i) == (2, 2):
                sib_arrived(1, 0)
                products(1)
            if (s, i) == (3, 0):
                weigh()
                weighted(0)
                contract(0)
            if (s, i) == (3, 1):
                weighted(1)
                contract(1)
            if (s, i) == (3, 2):
                sib_arrived(1, 1)
                amplitudes(2)
                contract(2)
            if (s, i) == (3, 3):
                sib_arrived(2, 0)
                amplitudes(3)
                contract(3)
            if (s, i) == (4, 0):
                sib_arrived(2, 1)
                amplitudes(4)
                contract(4)
            if (s, i) == (4, 1):
                sib_arrived(3, 0)
                amplitudes(5)
                for d, c in ((0, 0), (1, 3), (0, 1), (1, 2)):
                    copies.arrived(("d", d, c))
                    sib_send(4, 1, 0, c)
                contract(5)
    amplitudes(6)
    contract(6)
    sib_arrived(3, 1)
    sib_arrived(4, 0)
    sib_arrived(4, 1)
    amplitudes(7)

    def sliced(ref, which, to, rows):
        return ref.at[which * NY + to, pl.ds(rows.start, rows.stop - rows.start), :]

    contract_last(other, X_FIRST)
    copies.start(("x1", 0), sb_ref.at[pl.ds(other * NY, NY), pl.ds(0, 192), :], rx_ref, partner)
    for which in (0, 1):
        contract_last(which, Y_FIRST)
        for n, to in enumerate((y_r, y_l, y_o)):
            copies.start(("y1", n, which), sliced(sb_ref, which, to, Y_FIRST), ry_ref.at[n, which], ys[n])
    for which in (0, 1):
        contract_last(which, DIRECT)
    for n, who in enumerate(peers):
        copies.start(("r", n), sb_ref.at[who[1], pl.ds(384, 128), :], rd_ref.at[n], who)
    contract_last(x_hi, X_FIRST)

    copies.arrived(("x1", 0))
    for to in range(NY):
        t3_ref[to] = (acc_ref[x_hi * NY + to, X_FIRST, :] + rx_ref[to].astype(F32)).astype(BF16)
    for n, to in enumerate((y_r, y_l, y_o)):
        copies.start(("y2", n), t3_ref.at[to], ry2_ref.at[n], ys[n])

    stores = []

    def store(rows):
        part = pl.ds(rows.start, rows.stop - rows.start)
        copy = pltpu.make_async_copy(out_ref.at[part, :], out_hbm.at[0, part, :], local_sem.at[5 + len(stores)])
        copy.start()
        return copy

    def y_sum(which):
        total = acc_ref[which * NY + y, Y_FIRST, :]
        for n in range(3):
            total = total + ry_ref[n, which].astype(F32)
        return total

    for n in range(3):
        for which in (0, 1):
            copies.arrived(("y1", n, which))
    t2_ref[...] = y_sum(other).astype(BF16)
    copies.start(("x2", 0), t2_ref, rx2_ref, partner)
    total = acc_ref[rep, DIRECT, :]
    for n in range(7):
        copies.arrived(("r", n))
        total = total + rd_ref[n].astype(F32)
    out_ref[DIRECT, :] = total
    stores.append(store(DIRECT))
    total = acc_ref[rep, X_FIRST, :] + rx_ref[y].astype(F32)
    for n in range(3):
        copies.arrived(("y2", n))
        total = total + ry2_ref[n].astype(F32)
    out_ref[X_FIRST, :] = total
    stores.append(store(X_FIRST))
    total = y_sum(x_hi)
    copies.arrived(("x2", 0))
    out_ref[Y_FIRST, :] = total + rx2_ref[...].astype(F32)
    stores.append(store(Y_FIRST))
    for copy in stores:
        copy.wait()
    copies.finish()


def per_device(integrals, eps_occ, eps_vir, offsets):
    v, aux = integrals.shape[1:]
    n_x, n_y, n_d = (part.stop - part.start for part in (X_FIRST, Y_FIRST, DIRECT))
    anywhere = pl.BlockSpec(memory_space=pl.ANY)
    return pl.pallas_call(
        kernel,
        out_shape=jax.ShapeDtypeStruct((1, v, aux // 8), F32),
        in_specs=[anywhere] * 4,
        out_specs=anywhere,
        scratch_shapes=[
            pltpu.VMEM((v, aux), BF16),
            pltpu.VMEM((1, v), F32),
            pltpu.SMEM((ORBS,), F32),
            pltpu.SMEM((2,), jnp.int32),
            pltpu.VMEM((v, aux // 8), F32),
            pltpu.VMEM((2048, aux), BF16),
            pltpu.VMEM((v, 2048), F32),
            pltpu.VMEM((1, 2048), F32),
            pltpu.VMEM((1, 2048), F32),
            pltpu.VMEM((v, 128), F32),
            pltpu.VMEM((2, v, BLOCK), BF16),
            pltpu.VMEM((8, v, 128), F32),
            pltpu.VMEM((8, v, 128), BF16),
            pltpu.VMEM((8, 8, 128), jnp.int32),
            pltpu.VMEM((7, n_d, 128), BF16),
            pltpu.VMEM((NY, n_x, 128), BF16),
            pltpu.VMEM((3, 2, n_y, 128), BF16),
            pltpu.VMEM((NY, n_x, 128), BF16),
            pltpu.VMEM((3, n_x, 128), BF16),
            pltpu.VMEM((n_y, 128), BF16),
            pltpu.VMEM((n_y, 128), BF16),
            pltpu.SemaphoreType.DMA((N_COPIES,)),
            pltpu.SemaphoreType.DMA((N_COPIES,)),
            pltpu.SemaphoreType.DMA((8,)),
        ],
        compiler_params=pltpu.CompilerParams(
            collective_id=0, has_side_effects=True, vmem_limit_bytes=54784 << 10
        ),
        name="pair_amplitudes",
    )(integrals[0], eps_vir[None, :], eps_occ, offsets)


def solution(mesh):
    in_specs = (P("blk", None, None), P(), P(), P("rep"))
    out_specs = P("blk", None, "rep")
    return jax.shard_map(
        per_device, mesh=mesh, in_specs=in_specs, out_specs=out_specs, check_vma=False
    )
```

```python
import jax
import jax.numpy as jnp
from jax import lax
from jax.experimental import pallas as pl
from jax.experimental.pallas import tpu as pltpu
from jax.sharding import PartitionSpec as P

MESH = pl.DeviceIdType.MESH
F32 = jnp.float32
BF16 = jnp.bfloat16

NZ, NY, NX = 8, 4, 4
ORBS = 32
PIECE = 32
BLOCK = 256
X_FIRST, Y_FIRST, DIRECT = slice(0, 192), slice(192, 384), slice(384, 512)


def row_of(g, rel, kind, par, q):
    if g == 4:
        return 1664 + 256 * rel + (kind * 2 + par) * PIECE
    if g == 0:
        return (kind * 2 + par) * 64 + PIECE * q
    if g == 3 and kind == 1:
        return 1536 + 256 * rel + 64 * par + PIECE * q
    return (4 + (g - 1) * 8 + kind * 4 + rel * 2 + par) * 64 + PIECE * q


class Copies:
    def __init__(self, send_sem, recv_sem):
        self.send_sem, self.recv_sem = send_sem, recv_sem
        self.made = {}

    def start(self, name, src, dst, device, recv=None):
        n = len(self.made)
        copy = pltpu.make_async_remote_copy(
            src_ref=src, dst_ref=dst, send_sem=self.send_sem.at[n],
            recv_sem=self.recv_sem.at[n + 4 if recv is None else recv],
            device_id=device, device_id_type=MESH,
        )
        self.made[name] = copy
        copy.start()

    def arrived(self, name):
        self.made[name].wait_recv()

    def finish(self, names):
        for name in names:
            self.made[name].wait_send()


N_COPIES = 112


def kernel(b_hbm, ev_hbm, eo_hbm, off_hbm, out_hbm, b_ref, ev_ref, eo_ref, off_ref, out_ref, g_ref, inv_ref, ct_ref, w_ref, evc_ref, amp_ref,
           acc_ref, sb_ref, offb_ref, rd_ref, rx_ref, ry_ref, t3_ref, ry2_ref, t2_ref, rx2_ref, send_sem, recv_sem, local_sem):
    blk = lax.axis_index("blk")
    rep = lax.axis_index("rep")
    core = lax.rem(blk, 2)
    z = lax.rem(lax.div(blk, 2), NZ)
    x_lo = lax.div(blk, 2 * NZ)
    y = lax.rem(rep, NY)
    x_hi = lax.div(rep, NY)
    x = 2 * x_hi + x_lo
    other = 1 - x_hi

    def device(xx, zz, cc):
        return (lax.rem(xx, 2) * (2 * NZ) + zz * 2 + cc, lax.div(xx, 2) * NY + y)

    x_r, x_l = lax.rem(x + 1, NX), lax.rem(x + NX - 1, NX)
    z_r, z_l = lax.rem(z + 1, NZ), lax.rem(z + NZ - 1, NZ)
    xs = (device(x_r, z, core), device(x_l, z, core))
    z_f = lax.rem(z + 1 + (NZ - 2) * core, NZ)
    onward = device(x, z_f, core)
    x_f, x_s = lax.rem(x + 1 + 2 * core, NX), lax.rem(x + 3 - 2 * core, NX)
    sideways = (device(x_f, z, core), device(x_s, z, core))
    diagonal = device(x_f, z_f, core)
    sib = device(x, z, 1 - core)
    y_r, y_l, y_o = lax.rem(y + 1, NY), lax.rem(y + NY - 1, NY), lax.rem(y + 2, NY)
    ys = ((blk, x_hi * NY + y_r), (blk, x_hi * NY + y_l), (blk, x_hi * NY + y_o))
    partner = (blk, other * NY + y)
    peers = []
    for dx in (1, 0):
        for dy in (2, 1, 3, 0):
            if dx or dy:
                to = lax.rem(y + dy, NY)
                xh = other if dx else x_hi
                peers.append((blk, xh * NY + to))

    loads = []
    for n, (src, dst) in enumerate(((off_hbm, off_ref), (b_hbm, b_ref), (ev_hbm, ev_ref), (eo_hbm, eo_ref))):
        loads.append(pltpu.make_async_copy(src, dst, local_sem.at[1 + n]))

    barrier = pltpu.get_barrier_semaphore()
    around = [device(x, zz, cc) for zz in (z_r, z_l) for cc in (0, 1)]
    greeted = (*around, *xs, *ys[:2], sib)
    for who in greeted:
        pl.semaphore_signal(barrier, inc=1, device_id=who, device_id_type=MESH)
    for load in loads:
        load.start()
    loads[0].wait()
    rows8 = lax.broadcasted_iota(jnp.int32, (8, 128), 0)
    offb_ref[0] = jnp.where(rows8 == 0, off_ref[0], jnp.where(rows8 == 1, off_ref[1], -1))
    loads[1].wait()
    pl.semaphore_wait(barrier, len(greeted))

    copies = Copies(send_sem, recv_sem)
    mine = pl.multiple_of(128 * y + 64 * x_hi, 64)

    def half(i):
        return i + core * (1 - 2 * i)

    def slot(g, rel, kind, par, q, rows=PIECE):
        start = row_of(g, rel, kind, par, q)
        return g_ref.at[pl.ds(start if isinstance(start, int) else pl.multiple_of(start, PIECE), rows), :]

    def own(q, rows=PIECE):
        return b_ref.at[pl.ds(mine + PIECE * q, rows), :]

    def z_send(s, par, i):
        copies.start(("z", s, par, i), slot(s, 0, 0, par, half(i)), slot(s + 1, 0, 0, par, half(i)), onward)

    def x_send(s, par, i):
        copies.start(("x", s, par, i), slot(s, 0, 0, par, half(i)), slot(s, 0, 1, par, half(i)), sideways[i])

    def sib_send(g, kind, par, i):
        copies.start(("s", g, kind, par, i), slot(g, 0, kind, par, half(i)), slot(g, 1, kind, par, half(i)), sib)

    for n in range(2):
        copies.start(("o", n), offb_ref.at[0], offb_ref.at[1 + n], ys[n])
    for i in range(2):
        for d, to in enumerate((device(x, z_r, 0), device(x, z_l, 1))):
            q = 1 - i if d else i
            copies.start(("z", 0, d, i), own(q), slot(1, 0, 0, core, q), to, recv=core * 2 + i)
    for q in range(2):
        copies.start(("x", 0, q), own(q), slot(0, 0, 1, 0, q), xs[q])
    copies.start(("s", 0, 0), own(0, 64), slot(0, 0, 0, 1, 0, 64), sib)
    local = pltpu.make_async_copy(own(0, 64), slot(0, 0, 0, 0, 0, 64), local_sem.at[0])
    local.start()

    loads[2].wait()
    loads[3].wait()
    lanes = lax.broadcasted_iota(jnp.int32, (1, 128), 1)
    ev_y = ev_ref[:, pl.ds(pl.multiple_of(128 * y, 128), 128)]
    turned = [ev_y] + [jnp.concatenate([ev_y[:, 32 * t:], ev_y[:, :32 * t]], axis=1) for t in (1, 2, 3)]
    chunk = lax.div(lanes, PIECE)
    e_k = eo_ref[blk]
    from_left, from_right = 2 * lax.div(x_l, 2), 2 * lax.div(x_r, 2) + 1

    def orbital(kind, dz, par):
        xl = x_lo if kind == 0 else 1 - x_lo
        return xl * (2 * NZ) + lax.rem(z + dz + NZ, NZ) * 2 + par

    runs = [None] * 64
    for kind in range(2):
        quarters = (2 * x_hi, 2 * x_hi + 1) if kind == 0 else (from_left, from_right)
        for rel in range(2):
            toward = 2 * core - 1 if rel == 0 else 1 - 2 * core
            for par in range(2):
                for g in (1, 2, 3):
                    for q in range(2):
                        runs[row_of(g, rel, kind, par, q) // PIECE] = (orbital(kind, g * toward, par), quarters[q])
                q = core if rel == 0 else 1 - core
                runs[row_of(4, rel, kind, par, 0) // PIECE] = (
                    orbital(kind, 4, par), quarters[0] + q * (quarters[1] - quarters[0]))
        for par in range(2):
            for q in range(2):
                runs[row_of(0, 0, kind, par, q) // PIECE] = (
                    orbital(kind, 0, core if par == 0 else 1 - core), quarters[q])

    def by_chunk(values):
        first = jnp.where(chunk == 0, values[0], values[1])
        return jnp.where(chunk < 2, first, jnp.where(chunk == 2, values[2], values[3]))

    distances = []
    for n in range(0, 64, 4):
        e_l, dist, turn = [], [], []
        for place, (orb, quarter) in enumerate(runs[n:n + 4]):
            gap = lax.rem(blk - orb + ORBS, ORBS)
            e_l.append(eo_ref[orb])
            dist.append(jnp.minimum(gap, ORBS - gap))
            turn.append(lax.rem(quarter + 4 - place, 4))
        turn = by_chunk(turn)
        ev_b = jnp.where(turn == 0, turned[0], jnp.where(turn == 1, turned[1], jnp.where(turn == 2, turned[2], turned[3])))
        ct_ref[:, PIECE * n:PIECE * n + 128] = ev_b - e_k - by_chunk(e_l)
        distances.append((PIECE * n, by_chunk(dist)))
    for n in range(4):
        tile = jnp.broadcast_to(ev_ref[:, 128 * n:128 * n + 128], (128, 128))
        evc_ref[128 * n:128 * n + 128, :] = tile.T

    def invert(i, carry):
        rows = pl.ds(pl.multiple_of(i * 32, 32), 32)
        ev_a = evc_ref[rows, :]
        for n in range(16):
            cols = slice(128 * n, 128 * n + 128)
            inv_ref[rows, cols] = -1.0 / (ev_a + ct_ref[:, cols])
        return carry

    lax.fori_loop(0, 16, invert, 0)

    def weigh():
        copies.arrived(("o", 3))
        table = offb_ref[...].reshape(64, 128)
        for col, dist in distances:
            count = jnp.sum(jnp.where(table == dist, 1.0, 0.0), axis=0, keepdims=True)
            w_ref[:, col:col + 128] = jnp.where(dist == 0, 2.0 * count, count)

    def amplitudes(n, parts=(slice(0, 256), slice(256, 512))):
        cols = slice(BLOCK * n, BLOCK * n + BLOCK)
        right = g_ref[cols, :]
        weight = w_ref[:, cols]
        for rows in parts:
            pair = lax.dot_general(b_ref[rows, :], right, (((1,), (1,)), ((), ())),
                                   preferred_element_type=F32)
            amp_ref[n % 2, rows, :] = (pair * (inv_ref[rows, cols] * weight)).astype(BF16)

    def products(n):
        cols = slice(BLOCK * n, BLOCK * n + BLOCK)
        right = g_ref[cols, :]
        for m in range(2):
            rows = slice(256 * m, 256 * m + 256)
            pair = lax.dot_general(b_ref[rows, :], right, (((1,), (1,)), ((), ())),
                                   preferred_element_type=F32)
            inv_ref[rows, cols] = pair * inv_ref[rows, cols]

    def weighted(n):
        cols = slice(BLOCK * n, BLOCK * n + BLOCK)
        amp_ref[n % 2] = (inv_ref[:, cols] * w_ref[:, cols]).astype(BF16)

    def contract(n):
        for m in range(4):
            res = jnp.dot(amp_ref[n % 2], g_ref[BLOCK * n:BLOCK * n + BLOCK, 256 * m:256 * m + 256],
                          preferred_element_type=F32)
            for h in range(2):
                val = res[:, 128 * h:128 * h + 128]
                if n > 0:
                    val = val + acc_ref[2 * m + h]
                acc_ref[2 * m + h] = val

    def contract_last(which, rows):
        for m in range(2):
            cols = pl.ds(pl.multiple_of(which * 512 + 256 * m, 256), 256)
            res = jnp.dot(amp_ref[1, rows, :], g_ref[7 * BLOCK:, cols], preferred_element_type=F32)
            for h in range(2):
                j = which * NY + 2 * m + h
                val = res[:, 128 * h:128 * h + 128] + acc_ref[j, rows, :]
                acc_ref[j, rows, :] = val
                sb_ref[j, rows, :] = val.astype(BF16)

    def sib_arrived(g, kind):
        if g == 0:
            copies.arrived(("s", 0, kind))
            return
        for i in range(2 if g < 4 else 1):
            for par in range(2):
                copies.arrived(("s", g, kind, par, i))

    def x_arrivals(g, j):
        copies.arrived(("x", g, j % 2, j // 2))
        sib_send(g, 1, j % 2, j // 2)

    copies.arrived(("o", 0))
    copies.start(("o", 2), offb_ref.at[1], offb_ref.at[3], ys[0])
    for s in range(1, 5):
        for i in range(4 if s < 4 else 2):
            part, par = i // 2, i % 2
            if s == 1:
                piece = slot(1, 0, 0, par, half(part))
                pltpu.make_async_remote_copy(
                    src_ref=piece, dst_ref=piece, send_sem=send_sem.at[0], recv_sem=recv_sem.at[par * 2 + part],
                    device_id=onward, device_id_type=MESH,
                ).wait_recv()
            else:
                copies.arrived(("z", s - 1, par, part))
            if s < 3 or (s == 3 and part == 0):
                z_send(s, par, part)
            if s == 3 and part == 0:
                copies.start(("d", par), slot(3, 0, 0, par, half(0)), slot(4, 0, 1, par, 0), diagonal)
            if s < 4:
                x_send(s, par, part)
            sib_send(s, 0, par, part)
            if s == 1 and i == 1:
                for q in range(2):
                    copies.arrived(("x", 0, q))
                copies.start(("s", 0, 1), slot(0, 0, 1, 0, 0, 64), slot(0, 0, 1, 1, 0, 64), sib)
            if s in (2, 3) and i > 0:
                x_arrivals(s - 1, i - 1)
            if s in (2, 3) and i == 3:
                x_arrivals(s - 1, 3)
            if s == 4:
                copies.arrived(("d", par))
                sib_send(4, 1, par, 0)
            if (s, i) == (4, 0):
                x_arrivals(3, 0)
                x_arrivals(3, 1)
            if (s, i) == (1, 3):
                copies.arrived(("o", 1))
                copies.arrived(("o", 2))
                copies.start(("o", 3), offb_ref.at[pl.ds(0, 4)], offb_ref.at[pl.ds(4, 4)], partner)
            if (s, i) == (2, 0):
                sib_arrived(0, 0)
                sib_arrived(0, 1)
                local.wait()
                products(0)
            if (s, i) == (2, 2):
                sib_arrived(1, 0)
                products(1)
            if (s, i) == (3, 0):
                weigh()
                weighted(0)
                contract(0)
            if (s, i) == (3, 1):
                weighted(1)
                contract(1)
            if (s, i) == (3, 2):
                sib_arrived(1, 1)
                amplitudes(2)
                contract(2)
            if (s, i) == (3, 3):
                sib_arrived(2, 0)
                amplitudes(3)
                contract(3)
            if (s, i) == (4, 0):
                sib_arrived(2, 1)
                amplitudes(4)
                contract(4)
            if (s, i) == (4, 1):
                sib_arrived(3, 0)
                amplitudes(5)
                x_arrivals(3, 2)
                x_arrivals(3, 3)
                contract(5)
    amplitudes(6)
    contract(6)
    sib_arrived(3, 1)
    sib_arrived(4, 0)
    sib_arrived(4, 1)

    gathers = list(copies.made)
    def sliced(ref, which, to, rows):
        return ref.at[which * NY + to, pl.ds(rows.start, rows.stop - rows.start), :]

    amplitudes(7, (X_FIRST,))
    contract_last(other, X_FIRST)
    copies.start(("x1", 0), sb_ref.at[pl.ds(other * NY, NY), pl.ds(0, 192), :], rx_ref, partner)
    amplitudes(7, (Y_FIRST,))
    for which in (0, 1):
        contract_last(which, Y_FIRST)
        for n, to in enumerate((y_r, y_l, y_o)):
            copies.start(("y1", n, which), sliced(sb_ref, which, to, Y_FIRST), ry_ref.at[n, which], ys[n])
    amplitudes(7, (DIRECT,))
    for which in (0, 1):
        contract_last(which, DIRECT)
    for n, who in enumerate(peers):
        copies.start(("r", n), sb_ref.at[who[1], pl.ds(384, 128), :], rd_ref.at[n], who)
    contract_last(x_hi, X_FIRST)
    copies.finish(gathers)

    copies.arrived(("x1", 0))
    for to in range(NY):
        t3_ref[to] = (acc_ref[x_hi * NY + to, X_FIRST, :] + rx_ref[to].astype(F32)).astype(BF16)
    for n, to in enumerate((y_r, y_l, y_o)):
        copies.start(("y2", n), t3_ref.at[to], ry2_ref.at[n], ys[n])

    stores = []

    def store(rows):
        part = pl.ds(rows.start, rows.stop - rows.start)
        copy = pltpu.make_async_copy(out_ref.at[part, :], out_hbm.at[0, part, :], local_sem.at[5 + len(stores)])
        copy.start()
        return copy

    def y_sum(which):
        total = acc_ref[which * NY + y, Y_FIRST, :]
        for n in range(3):
            total = total + ry_ref[n, which].astype(F32)
        return total

    for n in range(3):
        for which in (0, 1):
            copies.arrived(("y1", n, which))
    t2_ref[...] = y_sum(other).astype(BF16)
    copies.start(("x2", 0), t2_ref, rx2_ref, partner)
    total = acc_ref[rep, DIRECT, :]
    for n in range(7):
        copies.arrived(("r", n))
        total = total + rd_ref[n].astype(F32)
    out_ref[DIRECT, :] = total
    stores.append(store(DIRECT))
    total = acc_ref[rep, X_FIRST, :] + rx_ref[y].astype(F32)
    for n in range(3):
        copies.arrived(("y2", n))
        total = total + ry2_ref[n].astype(F32)
    out_ref[X_FIRST, :] = total
    stores.append(store(X_FIRST))
    total = y_sum(x_hi)
    copies.arrived(("x2", 0))
    out_ref[Y_FIRST, :] = total + rx2_ref[...].astype(F32)
    stores.append(store(Y_FIRST))
    for copy in stores:
        copy.wait()
    copies.finish([name for name in copies.made if name not in gathers])


def per_device(integrals, eps_occ, eps_vir, offsets):
    v, aux = integrals.shape[1:]
    n_x, n_y, n_d = (part.stop - part.start for part in (X_FIRST, Y_FIRST, DIRECT))
    anywhere = pl.BlockSpec(memory_space=pl.ANY)
    return pl.pallas_call(
        kernel,
        out_shape=jax.ShapeDtypeStruct((1, v, aux // 8), F32),
        in_specs=[anywhere] * 4,
        out_specs=anywhere,
        scratch_shapes=[
            pltpu.VMEM((v, aux), BF16),
            pltpu.VMEM((1, v), F32),
            pltpu.SMEM((ORBS,), F32),
            pltpu.SMEM((2,), jnp.int32),
            pltpu.VMEM((v, aux // 8), F32),
            pltpu.VMEM((2048, aux), BF16),
            pltpu.VMEM((v, 2048), F32),
            pltpu.VMEM((1, 2048), F32),
            pltpu.VMEM((1, 2048), F32),
            pltpu.VMEM((v, 128), F32),
            pltpu.VMEM((2, v, BLOCK), BF16),
            pltpu.VMEM((8, v, 128), F32),
            pltpu.VMEM((8, v, 128), BF16),
            pltpu.VMEM((8, 8, 128), jnp.int32),
            pltpu.VMEM((7, n_d, 128), BF16),
            pltpu.VMEM((NY, n_x, 128), BF16),
            pltpu.VMEM((3, 2, n_y, 128), BF16),
            pltpu.VMEM((NY, n_x, 128), BF16),
            pltpu.VMEM((3, n_x, 128), BF16),
            pltpu.VMEM((n_y, 128), BF16),
            pltpu.VMEM((n_y, 128), BF16),
            pltpu.SemaphoreType.DMA((N_COPIES,)),
            pltpu.SemaphoreType.DMA((N_COPIES,)),
            pltpu.SemaphoreType.DMA((8,)),
        ],
        compiler_params=pltpu.CompilerParams(
            collective_id=0, has_side_effects=True, vmem_limit_bytes=54784 << 10
        ),
        name="pair_amplitudes",
    )(integrals[0], eps_vir[None, :], eps_occ, offsets)


def solution(mesh):
    in_specs = (P("blk", None, None), P(), P(), P("rep"))
    out_specs = P("blk", None, "rep")
    return jax.shard_map(
        per_device, mesh=mesh, in_specs=in_specs, out_specs=out_specs, check_vma=False
    )
```

```python
import jax
import jax.numpy as jnp
from jax import lax
from jax.experimental import pallas as pl
from jax.experimental.pallas import tpu as pltpu
from jax.sharding import PartitionSpec as P

MESH = pl.DeviceIdType.MESH
F32 = jnp.float32
BF16 = jnp.bfloat16

NZ, NY, NX = 8, 4, 4
ORBS = 32
PIECE = 32
BLOCK = 256
X_FIRST, Y_FIRST, DIRECT = slice(0, 224), slice(224, 384), slice(384, 512)


def row_of(g, rel, kind, par, q):
    if g == 4:
        return 1664 + 256 * rel + (kind * 2 + par) * PIECE
    if g == 0:
        return (kind * 2 + par) * 64 + PIECE * q
    if g == 3 and kind == 1:
        return 1536 + 256 * rel + 64 * par + PIECE * q
    return (4 + (g - 1) * 8 + kind * 4 + rel * 2 + par) * 64 + PIECE * q


def span(rows):
    return pl.ds(rows.start, rows.stop - rows.start)


class Copies:
    def __init__(self, send_sem, recv_sem):
        self.send_sem, self.recv_sem = send_sem, recv_sem
        self.made = {}

    def start(self, name, src, dst, device, recv=None):
        n = len(self.made)
        copy = pltpu.make_async_remote_copy(
            src_ref=src, dst_ref=dst, send_sem=self.send_sem.at[n],
            recv_sem=self.recv_sem.at[n + 4 if recv is None else recv],
            device_id=device, device_id_type=MESH,
        )
        self.made[name] = copy
        copy.start()

    def arrived(self, name):
        self.made[name].wait_recv()

    def finish(self, names):
        for name in names:
            self.made[name].wait_send()


N_COPIES = 112


def kernel(b_hbm, ev_hbm, eo_hbm, off_hbm, out_hbm, b_ref, ev_ref, eo_ref, off_ref, out_ref, g_ref, inv_ref, ct_ref, w_ref, evc_ref, amp_ref,
           acc_ref, sb_ref, offb_ref, rd_ref, rx_ref, ry_ref, t3_ref, ry2_ref, t2_ref, rx2_ref, send_sem, recv_sem, local_sem):
    blk = lax.axis_index("blk")
    rep = lax.axis_index("rep")
    core = lax.rem(blk, 2)
    z = lax.rem(lax.div(blk, 2), NZ)
    x_lo = lax.div(blk, 2 * NZ)
    y = lax.rem(rep, NY)
    x_hi = lax.div(rep, NY)
    x = 2 * x_hi + x_lo
    other = 1 - x_hi

    def device(xx, zz, cc):
        return (lax.rem(xx, 2) * (2 * NZ) + zz * 2 + cc, lax.div(xx, 2) * NY + y)

    x_r, x_l = lax.rem(x + 1, NX), lax.rem(x + NX - 1, NX)
    z_r, z_l = lax.rem(z + 1, NZ), lax.rem(z + NZ - 1, NZ)
    xs = (device(x_r, z, core), device(x_l, z, core))
    z_f = lax.rem(z + 1 + (NZ - 2) * core, NZ)
    onward = device(x, z_f, core)
    x_f, x_s = lax.rem(x + 1 + 2 * core, NX), lax.rem(x + 3 - 2 * core, NX)
    sideways = (device(x_f, z, core), device(x_s, z, core))
    diagonal = device(x_f, z_f, core)
    sib = device(x, z, 1 - core)
    y_r, y_l, y_o = lax.rem(y + 1, NY), lax.rem(y + NY - 1, NY), lax.rem(y + 2, NY)
    ys = ((blk, x_hi * NY + y_r), (blk, x_hi * NY + y_l), (blk, x_hi * NY + y_o))
    partner = (blk, other * NY + y)
    peers = []
    for dx in (1, 0):
        for dy in (2, 1, 3, 0):
            if dx or dy:
                to = lax.rem(y + dy, NY)
                xh = other if dx else x_hi
                peers.append((blk, xh * NY + to))

    loads = []
    for n, (src, dst) in enumerate(((off_hbm, off_ref), (b_hbm, b_ref), (ev_hbm, ev_ref), (eo_hbm, eo_ref))):
        loads.append(pltpu.make_async_copy(src, dst, local_sem.at[1 + n]))

    barrier = pltpu.get_barrier_semaphore()
    around = [device(x, zz, cc) for zz in (z_r, z_l) for cc in (0, 1)]
    greeted = (*around, *xs, *ys[:2], sib)
    for who in greeted:
        pl.semaphore_signal(barrier, inc=1, device_id=who, device_id_type=MESH)
    for load in loads:
        load.start()
    loads[0].wait()
    rows8 = lax.broadcasted_iota(jnp.int32, (8, 128), 0)
    offb_ref[0] = jnp.where(rows8 == 0, off_ref[0], jnp.where(rows8 == 1, off_ref[1], -1))
    loads[1].wait()
    pl.semaphore_wait(barrier, len(greeted))

    copies = Copies(send_sem, recv_sem)
    mine = pl.multiple_of(128 * y + 64 * x_hi, 64)

    def half(i):
        return i + core * (1 - 2 * i)

    def slot(g, rel, kind, par, q, rows=PIECE):
        start = row_of(g, rel, kind, par, q)
        return g_ref.at[pl.ds(start if isinstance(start, int) else pl.multiple_of(start, PIECE), rows), :]

    def own(q, rows=PIECE):
        return b_ref.at[pl.ds(mine + PIECE * q, rows), :]

    def z_send(s, par, i):
        copies.start(("z", s, par, i), slot(s, 0, 0, par, half(i)), slot(s + 1, 0, 0, par, half(i)), onward)

    def x_send(s, par, i):
        copies.start(("x", s, par, i), slot(s, 0, 0, par, half(i)), slot(s, 0, 1, par, half(i)), sideways[i])

    def sib_send(g, kind, par, i):
        copies.start(("s", g, kind, par, i), slot(g, 0, kind, par, half(i)), slot(g, 1, kind, par, half(i)), sib)

    for n in range(2):
        copies.start(("o", n), offb_ref.at[0], offb_ref.at[1 + n], ys[n])
    for i in range(2):
        for d, to in enumerate((device(x, z_r, 0), device(x, z_l, 1))):
            q = 1 - i if d else i
            copies.start(("z", 0, d, i), own(q), slot(1, 0, 0, core, q), to, recv=core * 2 + i)
    for q in range(2):
        copies.start(("x", 0, q), own(q), slot(0, 0, 1, 0, q), xs[q])
    copies.start(("s", 0, 0), own(0, 64), slot(0, 0, 0, 1, 0, 64), sib)
    local = pltpu.make_async_copy(own(0, 64), slot(0, 0, 0, 0, 0, 64), local_sem.at[0])
    local.start()

    loads[2].wait()
    loads[3].wait()
    lanes = lax.broadcasted_iota(jnp.int32, (1, 128), 1)
    ev_y = ev_ref[:, pl.ds(pl.multiple_of(128 * y, 128), 128)]
    turned = [ev_y] + [jnp.concatenate([ev_y[:, 32 * t:], ev_y[:, :32 * t]], axis=1) for t in (1, 2, 3)]
    chunk = lax.div(lanes, PIECE)
    e_k = eo_ref[blk]
    from_left, from_right = 2 * lax.div(x_l, 2), 2 * lax.div(x_r, 2) + 1

    def orbital(kind, dz, par):
        xl = x_lo if kind == 0 else 1 - x_lo
        return xl * (2 * NZ) + lax.rem(z + dz + NZ, NZ) * 2 + par

    runs = [None] * 64
    for kind in range(2):
        quarters = (2 * x_hi, 2 * x_hi + 1) if kind == 0 else (from_left, from_right)
        for rel in range(2):
            toward = 2 * core - 1 if rel == 0 else 1 - 2 * core
            for par in range(2):
                for g in (1, 2, 3):
                    for q in range(2):
                        runs[row_of(g, rel, kind, par, q) // PIECE] = (orbital(kind, g * toward, par), quarters[q])
                q = core if rel == 0 else 1 - core
                runs[row_of(4, rel, kind, par, 0) // PIECE] = (
                    orbital(kind, 4, par), quarters[0] + q * (quarters[1] - quarters[0]))
        for par in range(2):
            for q in range(2):
                runs[row_of(0, 0, kind, par, q) // PIECE] = (
                    orbital(kind, 0, core if par == 0 else 1 - core), quarters[q])

    def by_chunk(values):
        first = jnp.where(chunk == 0, values[0], values[1])
        return jnp.where(chunk < 2, first, jnp.where(chunk == 2, values[2], values[3]))

    distances = []
    for n in range(0, 64, 4):
        e_l, dist, turn = [], [], []
        for place, (orb, quarter) in enumerate(runs[n:n + 4]):
            gap = lax.rem(blk - orb + ORBS, ORBS)
            e_l.append(eo_ref[orb])
            dist.append(jnp.minimum(gap, ORBS - gap))
            turn.append(lax.rem(quarter + 4 - place, 4))
        turn = by_chunk(turn)
        ev_b = jnp.where(turn == 0, turned[0], jnp.where(turn == 1, turned[1], jnp.where(turn == 2, turned[2], turned[3])))
        ct_ref[:, PIECE * n:PIECE * n + 128] = ev_b - e_k - by_chunk(e_l)
        distances.append((PIECE * n, by_chunk(dist)))
    for n in range(4):
        tile = jnp.broadcast_to(ev_ref[:, 128 * n:128 * n + 128], (128, 128))
        evc_ref[128 * n:128 * n + 128, :] = tile.T

    def invert(i, carry):
        rows = pl.ds(pl.multiple_of(i * 32, 32), 32)
        ev_a = evc_ref[rows, :]
        for n in range(16):
            cols = slice(128 * n, 128 * n + 128)
            inv_ref[rows, cols] = -1.0 / (ev_a + ct_ref[:, cols])
        return carry

    lax.fori_loop(0, 16, invert, 0)

    def weigh():
        copies.arrived(("o", 3))
        table = offb_ref[...].reshape(64, 128)
        for col, dist in distances:
            count = jnp.sum(jnp.where(table == dist, 1.0, 0.0), axis=0, keepdims=True)
            w_ref[:, col:col + 128] = jnp.where(dist == 0, 2.0 * count, count)

    def amplitudes(n, parts=(slice(0, 256), slice(256, 512))):
        cols = slice(BLOCK * n, BLOCK * n + BLOCK)
        right = g_ref[cols, :]
        weight = w_ref[:, cols]
        for rows in parts:
            pair = lax.dot_general(b_ref[rows, :], right, (((1,), (1,)), ((), ())),
                                   preferred_element_type=F32)
            amp_ref[n % 2, rows, :] = (pair * (inv_ref[rows, cols] * weight)).astype(BF16)

    def products(n):
        cols = slice(BLOCK * n, BLOCK * n + BLOCK)
        right = g_ref[cols, :]
        for m in range(2):
            rows = slice(256 * m, 256 * m + 256)
            pair = lax.dot_general(b_ref[rows, :], right, (((1,), (1,)), ((), ())),
                                   preferred_element_type=F32)
            inv_ref[rows, cols] = pair * inv_ref[rows, cols]

    def weighted(n):
        cols = slice(BLOCK * n, BLOCK * n + BLOCK)
        amp_ref[n % 2] = (inv_ref[:, cols] * w_ref[:, cols]).astype(BF16)

    def contract(n):
        for m in range(4):
            res = jnp.dot(amp_ref[n % 2], g_ref[BLOCK * n:BLOCK * n + BLOCK, 256 * m:256 * m + 256],
                          preferred_element_type=F32)
            for h in range(2):
                val = res[:, 128 * h:128 * h + 128]
                if n > 0:
                    val = val + acc_ref[2 * m + h]
                acc_ref[2 * m + h] = val

    def contract_last(which, rows):
        for m in range(2):
            cols = pl.ds(pl.multiple_of(which * 512 + 256 * m, 256), 256)
            res = jnp.dot(amp_ref[1, rows, :], g_ref[7 * BLOCK:, cols], preferred_element_type=F32)
            for h in range(2):
                j = which * NY + 2 * m + h
                val = res[:, 128 * h:128 * h + 128] + acc_ref[j, rows, :]
                acc_ref[j, rows, :] = val
                sb_ref[j, rows, :] = val.astype(BF16)

    def sib_arrived(g, kind):
        if g == 0:
            copies.arrived(("s", 0, kind))
            return
        for i in range(2 if g < 4 else 1):
            for par in range(2):
                copies.arrived(("s", g, kind, par, i))

    def x_arrivals(g, j):
        copies.arrived(("x", g, j % 2, j // 2))
        sib_send(g, 1, j % 2, j // 2)

    copies.arrived(("o", 0))
    copies.start(("o", 2), offb_ref.at[1], offb_ref.at[3], ys[0])
    for s in range(1, 5):
        for i in range(4 if s < 4 else 2):
            part, par = i // 2, i % 2
            if s == 1:
                piece = slot(1, 0, 0, par, half(part))
                pltpu.make_async_remote_copy(
                    src_ref=piece, dst_ref=piece, send_sem=send_sem.at[0], recv_sem=recv_sem.at[par * 2 + part],
                    device_id=onward, device_id_type=MESH,
                ).wait_recv()
            else:
                copies.arrived(("z", s - 1, par, part))
            if s < 3 or (s == 3 and part == 0):
                z_send(s, par, part)
            if s == 3 and part == 0:
                copies.start(("d", par), slot(3, 0, 0, par, half(0)), slot(4, 0, 1, par, 0), diagonal)
            if s < 4:
                x_send(s, par, part)
            sib_send(s, 0, par, part)
            if s == 1 and i == 1:
                for q in range(2):
                    copies.arrived(("x", 0, q))
                copies.start(("s", 0, 1), slot(0, 0, 1, 0, 0, 64), slot(0, 0, 1, 1, 0, 64), sib)
            if s in (2, 3) and i > 0:
                x_arrivals(s - 1, i - 1)
            if s in (2, 3) and i == 3:
                x_arrivals(s - 1, 3)
            if s == 4:
                copies.arrived(("d", par))
                sib_send(4, 1, par, 0)
            if (s, i) == (4, 0):
                x_arrivals(3, 0)
                x_arrivals(3, 1)
            if (s, i) == (1, 3):
                copies.arrived(("o", 1))
                copies.arrived(("o", 2))
                copies.start(("o", 3), offb_ref.at[pl.ds(0, 4)], offb_ref.at[pl.ds(4, 4)], partner)
            if (s, i) == (2, 0):
                sib_arrived(0, 0)
                sib_arrived(0, 1)
                local.wait()
                products(0)
            if (s, i) == (2, 2):
                sib_arrived(1, 0)
                products(1)
            if (s, i) == (2, 3):
                weigh()
                weighted(0)
                contract(0)
            if (s, i) == (3, 0):
                weighted(1)
                contract(1)
            if (s, i) == (3, 1):
                sib_arrived(1, 1)
                amplitudes(2)
                contract(2)
            if (s, i) == (3, 2):
                sib_arrived(2, 0)
                amplitudes(3)
                contract(3)
            if (s, i) == (4, 0):
                sib_arrived(2, 1)
                amplitudes(4)
                contract(4)
            if (s, i) == (4, 1):
                x_arrivals(3, 2)
                x_arrivals(3, 3)
                sib_arrived(3, 0)
                amplitudes(5)
                contract(5)
    amplitudes(6)
    contract(6)
    sib_arrived(3, 1)
    sib_arrived(4, 0)
    sib_arrived(4, 1)

    gathers = list(copies.made)
    def sliced(ref, which, to, rows):
        return ref.at[which * NY + to, span(rows), :]

    amplitudes(7, (X_FIRST,))
    contract_last(other, X_FIRST)
    copies.start(("x1", 0), sb_ref.at[pl.ds(other * NY, NY), span(X_FIRST), :], rx_ref, partner)
    amplitudes(7, (Y_FIRST,))
    for which in (0, 1):
        contract_last(which, Y_FIRST)
        for n, to in enumerate((y_r, y_l, y_o)):
            copies.start(("y1", n, which), sliced(sb_ref, which, to, Y_FIRST), ry_ref.at[n, which], ys[n])
    amplitudes(7, (DIRECT,))
    for which in (0, 1):
        contract_last(which, DIRECT)
    for n, who in enumerate(peers):
        copies.start(("r", n), sb_ref.at[who[1], span(DIRECT), :], rd_ref.at[n], who)
    contract_last(x_hi, X_FIRST)
    copies.finish(gathers)

    copies.arrived(("x1", 0))
    for to in range(NY):
        t3_ref[to] = (acc_ref[x_hi * NY + to, X_FIRST, :] + rx_ref[to].astype(F32)).astype(BF16)
    for n, to in enumerate((y_r, y_l, y_o)):
        copies.start(("y2", n), t3_ref.at[to], ry2_ref.at[n], ys[n])

    stores = []

    def store(rows):
        part = span(rows)
        copy = pltpu.make_async_copy(out_ref.at[part, :], out_hbm.at[0, part, :], local_sem.at[5 + len(stores)])
        copy.start()
        return copy

    def y_sum(which):
        total = acc_ref[which * NY + y, Y_FIRST, :]
        for n in range(3):
            total = total + ry_ref[n, which].astype(F32)
        return total

    for n in range(3):
        for which in (0, 1):
            copies.arrived(("y1", n, which))
    t2_ref[...] = y_sum(other).astype(BF16)
    copies.start(("x2", 0), t2_ref, rx2_ref, partner)
    total = acc_ref[rep, DIRECT, :]
    for n in range(7):
        copies.arrived(("r", n))
        total = total + rd_ref[n].astype(F32)
    out_ref[DIRECT, :] = total
    stores.append(store(DIRECT))
    total = acc_ref[rep, X_FIRST, :] + rx_ref[y].astype(F32)
    for n in range(3):
        copies.arrived(("y2", n))
        total = total + ry2_ref[n].astype(F32)
    out_ref[X_FIRST, :] = total
    stores.append(store(X_FIRST))
    total = y_sum(x_hi)
    copies.arrived(("x2", 0))
    out_ref[Y_FIRST, :] = total + rx2_ref[...].astype(F32)
    stores.append(store(Y_FIRST))
    for copy in stores:
        copy.wait()
    copies.finish([name for name in copies.made if name not in gathers])


def per_device(integrals, eps_occ, eps_vir, offsets):
    v, aux = integrals.shape[1:]
    n_x, n_y, n_d = (part.stop - part.start for part in (X_FIRST, Y_FIRST, DIRECT))
    anywhere = pl.BlockSpec(memory_space=pl.ANY)
    return pl.pallas_call(
        kernel,
        out_shape=jax.ShapeDtypeStruct((1, v, aux // 8), F32),
        in_specs=[anywhere] * 4,
        out_specs=anywhere,
        scratch_shapes=[
            pltpu.VMEM((v, aux), BF16),
            pltpu.VMEM((1, v), F32),
            pltpu.SMEM((ORBS,), F32),
            pltpu.SMEM((2,), jnp.int32),
            pltpu.VMEM((v, aux // 8), F32),
            pltpu.VMEM((2048, aux), BF16),
            pltpu.VMEM((v, 2048), F32),
            pltpu.VMEM((1, 2048), F32),
            pltpu.VMEM((1, 2048), F32),
            pltpu.VMEM((v, 128), F32),
            pltpu.VMEM((2, v, BLOCK), BF16),
            pltpu.VMEM((8, v, 128), F32),
            pltpu.VMEM((8, v, 128), BF16),
            pltpu.VMEM((8, 8, 128), jnp.int32),
            pltpu.VMEM((7, n_d, 128), BF16),
            pltpu.VMEM((NY, n_x, 128), BF16),
            pltpu.VMEM((3, 2, n_y, 128), BF16),
            pltpu.VMEM((NY, n_x, 128), BF16),
            pltpu.VMEM((3, n_x, 128), BF16),
            pltpu.VMEM((n_y, 128), BF16),
            pltpu.VMEM((n_y, 128), BF16),
            pltpu.SemaphoreType.DMA((N_COPIES,)),
            pltpu.SemaphoreType.DMA((N_COPIES,)),
            pltpu.SemaphoreType.DMA((8,)),
        ],
        compiler_params=pltpu.CompilerParams(
            collective_id=0, has_side_effects=True, vmem_limit_bytes=24 << 20
        ),
        name="pair_amplitudes",
    )(*[pltpu.with_memory_space_constraint(arg, pltpu.HBM) for arg in (integrals[0], eps_vir[None, :], eps_occ, offsets)])


def solution(mesh):
    in_specs = (P("blk", None, None), P(), P(), P("rep"))
    out_specs = P("blk", None, "rep")
    return jax.shard_map(
        per_device, mesh=mesh, in_specs=in_specs, out_specs=out_specs, check_vma=False
    )
```

```python
import jax
import jax.numpy as jnp
from jax import lax
from jax.experimental import pallas as pl
from jax.experimental.pallas import tpu as pltpu
from jax.sharding import PartitionSpec as P

MESH = pl.DeviceIdType.MESH
F32 = jnp.float32
BF16 = jnp.bfloat16

NZ, NY, NX = 8, 4, 4
ORBS = 32
PIECE = 32
BLOCK = 256
X_FIRST, Y_FIRST, DIRECT = slice(0, 224), slice(224, 384), slice(384, 512)


def row_of(g, rel, kind, par, q):
    if g == 4:
        return 1664 + 256 * rel + (kind * 2 + par) * PIECE
    if g == 0:
        return (kind * 2 + par) * 64 + PIECE * q
    if g == 3 and kind == 1:
        return 1536 + 256 * rel + 64 * par + PIECE * q
    return (4 + (g - 1) * 8 + kind * 4 + rel * 2 + par) * 64 + PIECE * q


def span(rows):
    return pl.ds(rows.start, rows.stop - rows.start)


class Copies:
    def __init__(self, send_sem, recv_sem):
        self.send_sem, self.recv_sem = send_sem, recv_sem
        self.made = {}

    def start(self, name, src, dst, device, recv=None):
        n = len(self.made)
        copy = pltpu.make_async_remote_copy(
            src_ref=src, dst_ref=dst, send_sem=self.send_sem.at[n],
            recv_sem=self.recv_sem.at[n + 4 if recv is None else recv],
            device_id=device, device_id_type=MESH,
        )
        self.made[name] = copy
        copy.start()

    def arrived(self, name):
        self.made[name].wait_recv()

    def finish(self, names):
        for name in names:
            self.made[name].wait_send()


N_COPIES = 112


def kernel(b_hbm, ev_hbm, eo_hbm, off_hbm, out_hbm, b_ref, ev_ref, eo_ref, off_ref, out_ref, g_ref, inv_ref, ct_ref, w_ref, evc_ref, amp_ref,
           acc_ref, sb_ref, offb_ref, rd_ref, rx_ref, ry_ref, t3_ref, ry2_ref, t2_ref, rx2_ref, send_sem, recv_sem, local_sem):
    blk = lax.axis_index("blk")
    rep = lax.axis_index("rep")
    core = lax.rem(blk, 2)
    z = lax.rem(lax.div(blk, 2), NZ)
    x_lo = lax.div(blk, 2 * NZ)
    y = lax.rem(rep, NY)
    x_hi = lax.div(rep, NY)
    x = 2 * x_hi + x_lo
    other = 1 - x_hi

    def device(xx, zz, cc):
        return (lax.rem(xx, 2) * (2 * NZ) + zz * 2 + cc, lax.div(xx, 2) * NY + y)

    x_r, x_l = lax.rem(x + 1, NX), lax.rem(x + NX - 1, NX)
    z_r, z_l = lax.rem(z + 1, NZ), lax.rem(z + NZ - 1, NZ)
    xs = (device(x_r, z, core), device(x_l, z, core))
    z_f = lax.rem(z + 1 + (NZ - 2) * core, NZ)
    onward = device(x, z_f, core)
    x_f, x_s = lax.rem(x + 1 + 2 * core, NX), lax.rem(x + 3 - 2 * core, NX)
    sideways = (device(x_f, z, core), device(x_s, z, core))
    diagonal = device(x_f, z_f, core)
    sib = device(x, z, 1 - core)
    y_r, y_l, y_o = lax.rem(y + 1, NY), lax.rem(y + NY - 1, NY), lax.rem(y + 2, NY)
    ys = ((blk, x_hi * NY + y_r), (blk, x_hi * NY + y_l), (blk, x_hi * NY + y_o))
    partner = (blk, other * NY + y)
    peers = []
    for dx in (1, 0):
        for dy in (2, 1, 3, 0):
            if dx or dy:
                to = lax.rem(y + dy, NY)
                xh = other if dx else x_hi
                peers.append((blk, xh * NY + to))

    loads = []
    for n, (src, dst) in enumerate(((off_hbm, off_ref), (b_hbm, b_ref), (ev_hbm, ev_ref), (eo_hbm, eo_ref))):
        loads.append(pltpu.make_async_copy(src, dst, local_sem.at[1 + n]))

    barrier = pltpu.get_barrier_semaphore()
    around = [device(x, zz, cc) for zz in (z_r, z_l) for cc in (0, 1)]
    greeted = (*around, *xs, *ys[:2], sib)
    for who in greeted:
        pl.semaphore_signal(barrier, inc=1, device_id=who, device_id_type=MESH)
    for load in loads:
        load.start()
    loads[0].wait()
    rows8 = lax.broadcasted_iota(jnp.int32, (8, 128), 0)
    offb_ref[0] = jnp.where(rows8 == 0, off_ref[0], jnp.where(rows8 == 1, off_ref[1], -1))
    loads[1].wait()
    pl.semaphore_wait(barrier, len(greeted))

    copies = Copies(send_sem, recv_sem)
    mine = pl.multiple_of(128 * y + 64 * x_hi, 64)

    def half(i):
        return i + core * (1 - 2 * i)

    def slot(g, rel, kind, par, q, rows=PIECE):
        start = row_of(g, rel, kind, par, q)
        return g_ref.at[pl.ds(start if isinstance(start, int) else pl.multiple_of(start, PIECE), rows), :]

    def own(q, rows=PIECE):
        return b_ref.at[pl.ds(mine + PIECE * q, rows), :]

    def z_send(s, par, i):
        copies.start(("z", s, par, i), slot(s, 0, 0, par, half(i)), slot(s + 1, 0, 0, par, half(i)), onward)

    def x_send(s, par, i):
        copies.start(("x", s, par, i), slot(s, 0, 0, par, half(i)), slot(s, 0, 1, par, half(i)), sideways[i])

    def sib_send(g, kind, par, i):
        copies.start(("s", g, kind, par, i), slot(g, 0, kind, par, half(i)), slot(g, 1, kind, par, half(i)), sib)

    for n in range(2):
        copies.start(("o", n), offb_ref.at[0], offb_ref.at[1 + n], ys[n])
    for i in range(2):
        for d, to in enumerate((device(x, z_r, 0), device(x, z_l, 1))):
            q = 1 - i if d else i
            copies.start(("z", 0, d, i), own(q), slot(1, 0, 0, core, q), to, recv=core * 2 + i)
    for q in range(2):
        copies.start(("x", 0, q), own(q), slot(0, 0, 1, 0, q), xs[q])
    copies.start(("s", 0, 0), own(0, 64), slot(0, 0, 0, 1, 0, 64), sib)
    local = pltpu.make_async_copy(own(0, 64), slot(0, 0, 0, 0, 0, 64), local_sem.at[0])
    local.start()

    loads[2].wait()
    loads[3].wait()
    lanes = lax.broadcasted_iota(jnp.int32, (1, 128), 1)
    ev_y = ev_ref[:, pl.ds(pl.multiple_of(128 * y, 128), 128)]
    turned = [ev_y] + [jnp.concatenate([ev_y[:, 32 * t:], ev_y[:, :32 * t]], axis=1) for t in (1, 2, 3)]
    chunk = lax.div(lanes, PIECE)
    e_k = eo_ref[blk]
    from_left, from_right = 2 * lax.div(x_l, 2), 2 * lax.div(x_r, 2) + 1

    def orbital(kind, dz, par):
        xl = x_lo if kind == 0 else 1 - x_lo
        return xl * (2 * NZ) + lax.rem(z + dz + NZ, NZ) * 2 + par

    runs = [None] * 64
    for kind in range(2):
        quarters = (2 * x_hi, 2 * x_hi + 1) if kind == 0 else (from_left, from_right)
        for rel in range(2):
            toward = 2 * core - 1 if rel == 0 else 1 - 2 * core
            for par in range(2):
                for g in (1, 2, 3):
                    for q in range(2):
                        runs[row_of(g, rel, kind, par, q) // PIECE] = (orbital(kind, g * toward, par), quarters[q])
                q = core if rel == 0 else 1 - core
                runs[row_of(4, rel, kind, par, 0) // PIECE] = (
                    orbital(kind, 4, par), quarters[0] + q * (quarters[1] - quarters[0]))
        for par in range(2):
            for q in range(2):
                runs[row_of(0, 0, kind, par, q) // PIECE] = (
                    orbital(kind, 0, core if par == 0 else 1 - core), quarters[q])

    def by_chunk(values):
        first = jnp.where(chunk == 0, values[0], values[1])
        return jnp.where(chunk < 2, first, jnp.where(chunk == 2, values[2], values[3]))

    distances = []
    for n in range(0, 64, 4):
        e_l, dist, turn = [], [], []
        for place, (orb, quarter) in enumerate(runs[n:n + 4]):
            gap = lax.rem(blk - orb + ORBS, ORBS)
            e_l.append(eo_ref[orb])
            dist.append(jnp.minimum(gap, ORBS - gap))
            turn.append(lax.rem(quarter + 4 - place, 4))
        turn = by_chunk(turn)
        ev_b = jnp.where(turn == 0, turned[0], jnp.where(turn == 1, turned[1], jnp.where(turn == 2, turned[2], turned[3])))
        ct_ref[:, PIECE * n:PIECE * n + 128] = ev_b - e_k - by_chunk(e_l)
        distances.append((PIECE * n, by_chunk(dist)))
    for n in range(4):
        tile = jnp.broadcast_to(ev_ref[:, 128 * n:128 * n + 128], (128, 128))
        evc_ref[128 * n:128 * n + 128, :] = tile.T

    def invert(i, carry):
        rows = pl.ds(pl.multiple_of(i * 32, 32), 32)
        ev_a = evc_ref[rows, :]
        for n in range(16):
            cols = slice(128 * n, 128 * n + 128)
            inv_ref[rows, cols] = -1.0 / (ev_a + ct_ref[:, cols])
        return carry

    lax.fori_loop(0, 16, invert, 0)

    def weigh():
        copies.arrived(("o", 3))
        table = offb_ref[...].reshape(64, 128)
        for col, dist in distances:
            count = jnp.sum(jnp.where(table == dist, 1.0, 0.0), axis=0, keepdims=True)
            w_ref[:, col:col + 128] = jnp.where(dist == 0, 2.0 * count, count)

    def amplitudes(n, parts=(slice(0, 256), slice(256, 512))):
        cols = slice(BLOCK * n, BLOCK * n + BLOCK)
        right = g_ref[cols, :]
        weight = w_ref[:, cols]
        for rows in parts:
            pair = lax.dot_general(b_ref[rows, :], right, (((1,), (1,)), ((), ())),
                                   preferred_element_type=F32)
            amp_ref[n % 2, rows, :] = (pair * (inv_ref[rows, cols] * weight)).astype(BF16)

    def products(n):
        cols = slice(BLOCK * n, BLOCK * n + BLOCK)
        right = g_ref[cols, :]
        for m in range(2):
            rows = slice(256 * m, 256 * m + 256)
            pair = lax.dot_general(b_ref[rows, :], right, (((1,), (1,)), ((), ())),
                                   preferred_element_type=F32)
            inv_ref[rows, cols] = pair * inv_ref[rows, cols]

    def weighted(n):
        cols = slice(BLOCK * n, BLOCK * n + BLOCK)
        amp_ref[n % 2] = (inv_ref[:, cols] * w_ref[:, cols]).astype(BF16)

    def contract_two(n):
        for m in range(4):
            cols = slice(256 * m, 256 * m + 256)
            res = sum(jnp.dot(amp_ref[k], g_ref[BLOCK * (n + k):BLOCK * (n + k + 1), cols],
                              preferred_element_type=F32) for k in range(2))
            for h in range(2):
                val = res[:, 128 * h:128 * h + 128]
                if n > 0:
                    val = val + acc_ref[2 * m + h]
                acc_ref[2 * m + h] = val

    def contract_last(which, rows):
        for m in range(2):
            cols = pl.ds(pl.multiple_of(which * 512 + 256 * m, 256), 256)
            res = sum(jnp.dot(amp_ref[k, rows, :], g_ref[BLOCK * (6 + k):BLOCK * (7 + k), cols],
                              preferred_element_type=F32) for k in range(2))
            for h in range(2):
                j = which * NY + 2 * m + h
                val = res[:, 128 * h:128 * h + 128] + acc_ref[j, rows, :]
                acc_ref[j, rows, :] = val
                sb_ref[j, rows, :] = val.astype(BF16)

    def sib_arrived(g, kind):
        if g == 0:
            copies.arrived(("s", 0, kind))
            return
        for i in range(2 if g < 4 else 1):
            for par in range(2):
                copies.arrived(("s", g, kind, par, i))

    def x_arrivals(g, j):
        copies.arrived(("x", g, j % 2, j // 2))
        sib_send(g, 1, j % 2, j // 2)

    copies.arrived(("o", 0))
    copies.start(("o", 2), offb_ref.at[1], offb_ref.at[3], ys[0])
    for s in range(1, 5):
        for i in range(4 if s < 4 else 2):
            part, par = i // 2, i % 2
            if s == 1:
                piece = slot(1, 0, 0, par, half(part))
                pltpu.make_async_remote_copy(
                    src_ref=piece, dst_ref=piece, send_sem=send_sem.at[0], recv_sem=recv_sem.at[par * 2 + part],
                    device_id=onward, device_id_type=MESH,
                ).wait_recv()
            else:
                copies.arrived(("z", s - 1, par, part))
            if s < 3 or (s == 3 and part == 0):
                z_send(s, par, part)
            if s == 3 and part == 0:
                copies.start(("d", par), slot(3, 0, 0, par, half(0)), slot(4, 0, 1, par, 0), diagonal)
            if s < 4:
                x_send(s, par, part)
            sib_send(s, 0, par, part)
            if s == 1 and i == 1:
                for q in range(2):
                    copies.arrived(("x", 0, q))
                copies.start(("s", 0, 1), slot(0, 0, 1, 0, 0, 64), slot(0, 0, 1, 1, 0, 64), sib)
            if s in (2, 3) and i > 0:
                x_arrivals(s - 1, i - 1)
            if s in (2, 3) and i == 3:
                x_arrivals(s - 1, 3)
            if s == 4:
                copies.arrived(("d", par))
                sib_send(4, 1, par, 0)
            if (s, i) == (4, 0):
                x_arrivals(3, 0)
                x_arrivals(3, 1)
            if (s, i) == (1, 3):
                copies.arrived(("o", 1))
                copies.arrived(("o", 2))
                copies.start(("o", 3), offb_ref.at[pl.ds(0, 4)], offb_ref.at[pl.ds(4, 4)], partner)
            if (s, i) == (2, 0):
                sib_arrived(0, 0)
                sib_arrived(0, 1)
                local.wait()
                products(0)
            if (s, i) == (2, 2):
                sib_arrived(1, 0)
                products(1)
            if (s, i) == (2, 3):
                weigh()
                weighted(0)
                weighted(1)
            if (s, i) == (3, 0):
                contract_two(0)
            if (s, i) == (3, 1):
                sib_arrived(1, 1)
                amplitudes(2)
            if (s, i) == (3, 2):
                sib_arrived(2, 0)
                amplitudes(3)
                contract_two(2)
            if (s, i) == (4, 0):
                sib_arrived(2, 1)
                amplitudes(4)
            if (s, i) == (4, 1):
                x_arrivals(3, 2)
                x_arrivals(3, 3)
                sib_arrived(3, 0)
                amplitudes(5)
                contract_two(4)
    amplitudes(6)
    sib_arrived(3, 1)
    sib_arrived(4, 0)
    sib_arrived(4, 1)

    gathers = list(copies.made)
    def sliced(ref, which, to, rows):
        return ref.at[which * NY + to, span(rows), :]

    amplitudes(7, (X_FIRST,))
    contract_last(other, X_FIRST)
    copies.start(("x1", 0), sb_ref.at[pl.ds(other * NY, NY), span(X_FIRST), :], rx_ref, partner)
    amplitudes(7, (Y_FIRST,))
    for which in (0, 1):
        contract_last(which, Y_FIRST)
        for n, to in enumerate((y_r, y_l, y_o)):
            copies.start(("y1", n, which), sliced(sb_ref, which, to, Y_FIRST), ry_ref.at[n, which], ys[n])
    amplitudes(7, (DIRECT,))
    for which in (0, 1):
        contract_last(which, DIRECT)
    for n, who in enumerate(peers):
        copies.start(("r", n), sb_ref.at[who[1], span(DIRECT), :], rd_ref.at[n], who)
    contract_last(x_hi, X_FIRST)
    copies.finish(gathers)

    copies.arrived(("x1", 0))
    for to in range(NY):
        t3_ref[to] = (acc_ref[x_hi * NY + to, X_FIRST, :] + rx_ref[to].astype(F32)).astype(BF16)
    for n, to in enumerate((y_r, y_l, y_o)):
        copies.start(("y2", n), t3_ref.at[to], ry2_ref.at[n], ys[n])

    stores = []

    def store(rows):
        part = span(rows)
        copy = pltpu.make_async_copy(out_ref.at[part, :], out_hbm.at[0, part, :], local_sem.at[5 + len(stores)])
        copy.start()
        return copy

    def y_sum(which):
        total = acc_ref[which * NY + y, Y_FIRST, :]
        for n in range(3):
            total = total + ry_ref[n, which].astype(F32)
        return total

    for n in range(3):
        for which in (0, 1):
            copies.arrived(("y1", n, which))
    t2_ref[...] = y_sum(other).astype(BF16)
    copies.start(("x2", 0), t2_ref, rx2_ref, partner)
    total = acc_ref[rep, DIRECT, :]
    for n in range(7):
        copies.arrived(("r", n))
        total = total + rd_ref[n].astype(F32)
    out_ref[DIRECT, :] = total
    stores.append(store(DIRECT))
    total = acc_ref[rep, X_FIRST, :] + rx_ref[y].astype(F32)
    for n in range(3):
        copies.arrived(("y2", n))
        total = total + ry2_ref[n].astype(F32)
    out_ref[X_FIRST, :] = total
    stores.append(store(X_FIRST))
    total = y_sum(x_hi)
    copies.arrived(("x2", 0))
    out_ref[Y_FIRST, :] = total + rx2_ref[...].astype(F32)
    stores.append(store(Y_FIRST))
    for copy in stores:
        copy.wait()
    copies.finish([name for name in copies.made if name not in gathers])


def per_device(integrals, eps_occ, eps_vir, offsets):
    v, aux = integrals.shape[1:]
    n_x, n_y, n_d = (part.stop - part.start for part in (X_FIRST, Y_FIRST, DIRECT))
    anywhere = pl.BlockSpec(memory_space=pl.ANY)
    return pl.pallas_call(
        kernel,
        out_shape=jax.ShapeDtypeStruct((1, v, aux // 8), F32),
        in_specs=[anywhere] * 4,
        out_specs=anywhere,
        scratch_shapes=[
            pltpu.VMEM((v, aux), BF16),
            pltpu.VMEM((1, v), F32),
            pltpu.SMEM((ORBS,), F32),
            pltpu.SMEM((2,), jnp.int32),
            pltpu.VMEM((v, aux // 8), F32),
            pltpu.VMEM((2048, aux), BF16),
            pltpu.VMEM((v, 2048), F32),
            pltpu.VMEM((1, 2048), F32),
            pltpu.VMEM((1, 2048), F32),
            pltpu.VMEM((v, 128), F32),
            pltpu.VMEM((2, v, BLOCK), BF16),
            pltpu.VMEM((8, v, 128), F32),
            pltpu.VMEM((8, v, 128), BF16),
            pltpu.VMEM((8, 8, 128), jnp.int32),
            pltpu.VMEM((7, n_d, 128), BF16),
            pltpu.VMEM((NY, n_x, 128), BF16),
            pltpu.VMEM((3, 2, n_y, 128), BF16),
            pltpu.VMEM((NY, n_x, 128), BF16),
            pltpu.VMEM((3, n_x, 128), BF16),
            pltpu.VMEM((n_y, 128), BF16),
            pltpu.VMEM((n_y, 128), BF16),
            pltpu.SemaphoreType.DMA((N_COPIES,)),
            pltpu.SemaphoreType.DMA((N_COPIES,)),
            pltpu.SemaphoreType.DMA((8,)),
        ],
        compiler_params=pltpu.CompilerParams(
            collective_id=0, has_side_effects=True, vmem_limit_bytes=24 << 20
        ),
        name="pair_amplitudes",
    )(*[pltpu.with_memory_space_constraint(arg, pltpu.HBM) for arg in (integrals[0], eps_vir[None, :], eps_occ, offsets)])


def solution(mesh):
    in_specs = (P("blk", None, None), P(), P(), P("rep"))
    out_specs = P("blk", None, "rep")
    return jax.shard_map(
        per_device, mesh=mesh, in_specs=in_specs, out_specs=out_specs, check_vma=False
    )
```
